512 devices in a mesh: freq: 64 (over y, z), space: 8 (over x, core).
Axes of the slice: x: 4, y: 4, z: 16, core: 2. Of those that a mesh axis runs over, the one named last changes fastest.
Arguments:
- snapshots: bfloat16 [64, 256, 3, 2048], P('freq', None, None, 'space'), may hold values from -6 to 6
- point_weights: float32 [2048], P('space'), may hold values from 0.25 to 2
- owner_map: int32 [128], replicated, may hold values from 0 to 127, as said below
- triad_list: int32 [512, 2], replicated, may hold values from 0 to 127, as said below
Outputs:
- power_map: float32 [128, 2048], P('freq', 'space')
- coefficients: float32 [512, 2, 64], P('freq')
- modes: float32 [512, 2, 3, 2048], P('freq', None, None, 'space')
The draws below stay inside these ranges and needn't reach their ends.
Inputs may be any that keep to these rules, and one draw needn't show every extreme that they name: `owner_map`: A permutation of the 128 frequencies. triad_list[t, 0] + triad_list[t, 1] = owner_map[(t // 8) * 2 + t % 2], and triad_list[t, 0] = 0 when t % 8 == 0 or when that sum is 127.
All inputs are finite; a program needn't handle non-finite values.
Results may differ from the reference program's by a relative error of at most 0.005.
The reference program's roundings to bfloat16 on the way (of `dft_table`, `spectra`, `products` and `coef_rounded`) count: a program that leaves them out, or rounds other values in their place, can miss the bound.
Values may be sent and summed in bfloat16 or wider, within the bound.
A program may use at most 64 MiB of HBM per device.

```python
import math
import jax
import jax.numpy as jnp
from jax import lax

NFFT = 256
NF = 128
TRI_DEV = 8
NB = 64
NPTS = 2048
NT = 512


def owners_of(key):
    return jax.random.permutation(jax.random.fold_in(key, 11), NF).astype(jnp.int32)


def draw_owner_map(key, part):
    return owners_of(key)


def draw_triad_list(key, part):
    owners = owners_of(key)
    per_owner = NF // NB
    slots = jnp.arange(NT, dtype=jnp.int32)
    position = slots // TRI_DEV * per_owner + slots % per_owner
    totals = owners[position]
    raw = jax.random.randint(jax.random.fold_in(key, 12), (NT,), 0, NF, dtype=jnp.int32)
    first_freq = raw % (totals + 1)
    first_freq = jnp.where(slots % TRI_DEV == 0, 0, first_freq)
    first_freq = jnp.where(totals == NF - 1, 0, first_freq)
    second_freq = totals - first_freq
    return jnp.stack([first_freq, second_freq], axis=1).astype(jnp.int32)


def steps_of(stream_key, extent, pieces, smallest, top_value):
    gain = 1.0
    for axis_at, shards_of in pieces:
        draws = jax.random.uniform(jax.random.fold_in(jax.random.fold_in(stream_key, 6), axis_at), (shards_of,), jnp.float32, smallest / len(pieces), top_value / len(pieces))
        gain = gain * jnp.repeat(jnp.exp(draws), extent[axis_at] // shards_of).reshape((-1,) + (1,) * (len(extent) - 1 - axis_at))
    return gain


def normal_values(own_key, shape, spread, most, shards=(), held_as=jnp.bfloat16):
    factor_of = steps_of(own_key, shape, shards, -0.22, 0.18) if shards else 1.0
    result = jax.random.normal(own_key, shape, jnp.float32) * spread * factor_of
    return jnp.minimum(jnp.maximum(result, -most), most).astype(held_as)


def setup_inputs(seed: int = 0) -> dict:
    arg_keys = jax.random.split(jax.random.key(seed), 5)
    snapshots = normal_values(arg_keys[0], (NB, NFFT, 3, NPTS), 1.0, 6.0, ((0, 64), (3, 8)))
    point_weights = jnp.clip(jnp.exp(math.log(2.0) - 2.0794415 * jax.random.uniform(arg_keys[1], (NPTS,), jnp.float32) ** steps_of(arg_keys[1], (NPTS,), ((0, 8),), -0.2, 0.2)), 0.25, 2.0)
    owner_map = draw_owner_map(jax.random.fold_in(arg_keys[4], 71), 0)
    triad_list = draw_triad_list(jax.random.fold_in(arg_keys[4], 71), 0)
    return {"snapshots": snapshots, "point_weights": point_weights, "owner_map": owner_map, "triad_list": triad_list}


def make_table(samples, frequencies):
    sample_idx = jnp.arange(samples, dtype=jnp.int32)
    freq_idx = jnp.arange(frequencies, dtype=jnp.int32)
    angles = (freq_idx[:, None] * sample_idx[None, :] % samples).astype(jnp.float32) * (2.0 * math.pi / samples)
    window = 0.5 - 0.5 * jnp.cos(sample_idx.astype(jnp.float32) * (2.0 * math.pi / samples))
    taper = window / math.sqrt(samples)
    stacked = jnp.stack([jnp.cos(angles) * taper, -jnp.sin(angles) * taper], axis=1)
    return stacked.reshape(2 * frequencies, samples).astype(jnp.bfloat16)

def normalized(vec_real, vec_imag):
    energy = lax.optimization_barrier(jnp.mean(vec_real * vec_real + vec_imag * vec_imag, axis=-1, keepdims=True))
    factor = lax.rsqrt(energy + 1e-05)
    return (vec_real * factor, vec_imag * factor)

def leading_vector(gram_real, gram_imag):
    vec_real = jnp.ones(gram_real.shape[:-1], jnp.float32)
    vec_imag = jnp.zeros(gram_real.shape[:-1], jnp.float32)
    for sweep in range(2):
        next_real = jnp.einsum('...ij,...j->...i', gram_real, vec_real, precision=lax.Precision.HIGHEST) - jnp.einsum('...ij,...j->...i', gram_imag, vec_imag, precision=lax.Precision.HIGHEST)
        next_imag = jnp.einsum('...ij,...j->...i', gram_real, vec_imag, precision=lax.Precision.HIGHEST) + jnp.einsum('...ij,...j->...i', gram_imag, vec_real, precision=lax.Precision.HIGHEST)
        vec_real, vec_imag = normalized(next_real, next_imag)
    return (vec_real, vec_imag)

def reference(snapshots, point_weights, owner_map, triad_list):
    dft_table = make_table(NFFT, NF)

    def one_block(total, block):
        data = block.reshape(NFFT, 3 * NPTS)
        spec = jnp.dot(dft_table, data, preferred_element_type=jnp.float32).astype(jnp.bfloat16)
        spec = spec.reshape(NF, 2, 3, NPTS)
        spec_f = spec.astype(jnp.float32)
        return (total + lax.optimization_barrier(jnp.sum(spec_f * spec_f, axis=(1, 2))), spec)
    energy, spectra = lax.scan(one_block, jnp.zeros((NF, NPTS), jnp.float32), snapshots)
    power_map = jnp.take(energy / NB, owner_map.astype(jnp.int32), axis=0)
    point_weight = point_weights.astype(jnp.float32)

    def one_triad(freq_pair):
        first_freq = freq_pair[0].astype(jnp.int32)
        second_freq = freq_pair[1].astype(jnp.int32)
        first_rows = spectra[:, first_freq].astype(jnp.float32)
        second_rows = spectra[:, second_freq].astype(jnp.float32)
        sum_rows = spectra[:, first_freq + second_freq].astype(jnp.float32).reshape(NB, 2, 3 * NPTS)
        prod_real = (first_rows[:, 0] * second_rows[:, 0] - first_rows[:, 1] * second_rows[:, 1]) * point_weight
        prod_imag = (first_rows[:, 0] * second_rows[:, 1] + first_rows[:, 1] * second_rows[:, 0]) * point_weight
        products = jnp.stack([prod_real, prod_imag], axis=1).astype(jnp.bfloat16)
        products = lax.optimization_barrier(products).astype(jnp.float32).reshape(NB, 2, 3 * NPTS)
        gram_real = jnp.einsum('irc,jrc->ij', products, sum_rows, precision=lax.Precision.HIGHEST)
        gram_imag = jnp.einsum('ic,jc->ij', products[:, 0], sum_rows[:, 1], precision=lax.Precision.HIGHEST) - jnp.einsum('ic,jc->ij', products[:, 1], sum_rows[:, 0], precision=lax.Precision.HIGHEST)
        vec_real, vec_imag = leading_vector(gram_real, gram_imag)
        coef = jnp.stack([vec_real, vec_imag], axis=0)
        coef_rounded = lax.optimization_barrier(coef.astype(jnp.bfloat16)).astype(jnp.float32)
        mode_real = jnp.einsum('b,bc->c', coef_rounded[0], sum_rows[:, 0], precision=lax.Precision.HIGHEST) - jnp.einsum('b,bc->c', coef_rounded[1], sum_rows[:, 1], precision=lax.Precision.HIGHEST)
        mode_imag = jnp.einsum('b,bc->c', coef_rounded[0], sum_rows[:, 1], precision=lax.Precision.HIGHEST) + jnp.einsum('b,bc->c', coef_rounded[1], sum_rows[:, 0], precision=lax.Precision.HIGHEST)
        mode = jnp.stack([mode_real, mode_imag], axis=0) / math.sqrt(NB)
        return (coef, mode.reshape(2, 3, NPTS))
    coefficients, modes = lax.map(one_triad, triad_list)
    return (power_map, coefficients, modes)
```

```python
import math

import jax
import jax.numpy as jnp
from jax import lax
from jax.sharding import PartitionSpec as P


def make_table(samples, frequencies):
    sample_idx = jnp.arange(samples, dtype=jnp.int32)
    freq_idx = jnp.arange(frequencies, dtype=jnp.int32)
    angles = (freq_idx[:, None] * sample_idx[None, :] % samples).astype(jnp.float32) * (
        2.0 * math.pi / samples
    )
    window = 0.5 - 0.5 * jnp.cos(sample_idx.astype(jnp.float32) * (2.0 * math.pi / samples))
    taper = window / math.sqrt(samples)
    stacked = jnp.stack([jnp.cos(angles) * taper, -jnp.sin(angles) * taper], axis=1)
    return stacked.reshape(2 * frequencies, samples).astype(jnp.bfloat16)


def select_rows(index, rows):
    hot = (index[:, None] == jnp.arange(rows.shape[0], dtype=jnp.int32)[None, :]).astype(jnp.bfloat16)
    return jnp.dot(hot, rows, preferred_element_type=jnp.float32)


def sum_over_space(value):
    spread = jnp.broadcast_to(value[None], (lax.axis_size("space"),) + value.shape)
    return jnp.sum(lax.all_to_all(spread, "space", split_axis=0, concat_axis=0, tiled=True), axis=0)


def normalized(vec_real, vec_imag):
    energy = jnp.mean(vec_real * vec_real + vec_imag * vec_imag, axis=-1, keepdims=True)
    factor = lax.rsqrt(energy + 1e-05)
    return (vec_real * factor, vec_imag * factor)


def weighted_sum(vec_real, vec_imag, sums):
    both = jnp.concatenate([vec_real, vec_imag], axis=1)
    out = jnp.einsum(
        "sub,bsk->suk", both, sums, precision=lax.Precision.HIGHEST, preferred_element_type=jnp.float32
    )
    n, k = vec_real.shape[1], sums.shape[2] // 2
    real = out[:, :n, :k] - out[:, n:, k:]
    imag = out[:, :n, k:] + out[:, n:, :k]
    return (real, imag)


def body(snapshots, point_weights, owner_map, triad_list):
    samples = snapshots.shape[1]
    points = snapshots.shape[3]
    columns = 3 * points
    frequencies = owner_map.shape[0]
    triad_count = triad_list.shape[0]
    block_count = lax.axis_size("freq")
    triads_here = triad_count // block_count
    slots = frequencies // block_count
    dft_table = make_table(samples, frequencies)
    spectra = jnp.dot(
        dft_table, snapshots.reshape(samples, columns), preferred_element_type=jnp.float32
    ).astype(jnp.bfloat16)
    spectra = spectra.reshape(frequencies, 2 * columns)
    first = select_rows(triad_list[:, 0], spectra)
    second = select_rows(triad_list[:, 1], spectra)
    k_real, k_imag = first[:, :columns], first[:, columns:]
    l_real, l_imag = second[:, :columns], second[:, columns:]
    point_weight = jnp.tile(point_weights, 3)
    prod_real = ((k_real * l_real - k_imag * l_imag) * point_weight).astype(jnp.bfloat16)
    prod_imag = ((k_real * l_imag + k_imag * l_real) * point_weight).astype(jnp.bfloat16)
    products = jnp.concatenate([prod_real, prod_imag], axis=1)
    owned = select_rows(owner_map, spectra).astype(jnp.bfloat16)
    packet = jnp.concatenate(
        [
            products.reshape(block_count, triads_here, 2 * columns),
            owned.reshape(block_count, slots, 2 * columns),
        ],
        axis=1,
    )
    packet = lax.all_to_all(packet, "freq", split_axis=0, concat_axis=0, tiled=True)
    sums = packet[:, triads_here:]
    prods = packet[:, :triads_here].astype(jnp.float32)
    prods_real, prods_imag = prods[:, :, :columns], prods[:, :, columns:]
    sums_f = sums.astype(jnp.float32)
    power_map = jnp.sum((sums_f * sums_f).reshape(block_count, slots, 6, points), axis=(0, 2)) / block_count

    per_slot = triads_here // slots

    def apply(field_real, field_imag):
        v_real = jnp.sum(prods_real * field_real + prods_imag * field_imag, axis=2)
        v_imag = jnp.sum(prods_real * field_imag - prods_imag * field_real, axis=2)
        v = sum_over_space(jnp.stack([v_real.T, v_imag.T]))
        return normalized(v[0], v[1])

    def by_triad(x):
        return x.transpose(1, 0, 2).reshape(triads_here, columns)

    def by_slot(x):
        return x.reshape(per_slot, slots, block_count).transpose(1, 0, 2)

    total = jnp.sum(sums_f, axis=0)
    total = jnp.tile(total, (per_slot, 1))
    vec_real, vec_imag = apply(total[:, :columns], total[:, columns:])
    field_real, field_imag = weighted_sum(by_slot(vec_real), by_slot(vec_imag), sums_f)
    vec_real, vec_imag = apply(by_triad(field_real), by_triad(field_imag))
    coefficients = jnp.stack([vec_real, vec_imag], axis=1)
    rounded = lax.reduce_precision(coefficients, exponent_bits=8, mantissa_bits=7)
    mode_real, mode_imag = weighted_sum(by_slot(rounded[:, 0]), by_slot(rounded[:, 1]), sums_f)
    modes = jnp.stack([by_triad(mode_real), by_triad(mode_imag)], axis=1) / math.sqrt(block_count)
    return (power_map, coefficients, modes.reshape(triads_here, 2, 3, points))


def solution(mesh):
    placed = (P("freq", None, None, "space"), P("space"), P(), P())
    return jax.shard_map(
        body,
        mesh=mesh,
        in_specs=placed,
        out_specs=(P("freq", "space"), P("freq", None, None), P("freq", None, None, "space")),
        check_vma=False,
    )
```

```python
import functools
import math

import jax
import jax.numpy as jnp
from jax import lax
from jax.experimental import pallas as pl
from jax.experimental.pallas import tpu as pltpu
from jax.sharding import PartitionSpec as P


def make_table(samples, frequencies):
    sample_idx = jnp.arange(samples, dtype=jnp.int32)
    freq_idx = jnp.arange(frequencies, dtype=jnp.int32)
    angles = (freq_idx[:, None] * sample_idx[None, :] % samples).astype(jnp.float32) * (
        2.0 * math.pi / samples
    )
    window = 0.5 - 0.5 * jnp.cos(sample_idx.astype(jnp.float32) * (2.0 * math.pi / samples))
    taper = window / math.sqrt(samples)
    stacked = jnp.stack([jnp.cos(angles) * taper, -jnp.sin(angles) * taper], axis=1)
    return stacked.reshape(2 * frequencies, samples).astype(jnp.bfloat16)


def select_rows(index, rows):
    hot = (index[:, None] == jnp.arange(rows.shape[0], dtype=jnp.int32)[None, :]).astype(jnp.bfloat16)
    return jnp.dot(hot, rows, preferred_element_type=jnp.float32)


MESH = pl.DeviceIdType.MESH
LANES = 128


def kernel(
    nq, ne, spec_ref, own_ref, weight_ref, triad_ref,
    coef_ref, sums_ref,
    spec_all, flat, rows, prod_re, prod_im, sum_re, sum_im, field,
    part, part_in, piece, piece_in, mine, gathered, spread,
    send_sem, recv_sem,
):
    q = lax.axis_index("freq")
    e = lax.axis_index("space")
    blocks, cols, width = spec_ref.shape
    pad = flat.shape[1] // blocks
    triads = triad_ref.shape[1]
    per_e = blocks // ne
    groups = triads // LANES

    barrier = pltpu.get_barrier_semaphore()

    def others(axis, count, index, act):
        def step(i, carry):
            act({axis: lax.rem(index + i, count)}, lax.rem(index + i, count))
            return carry

        lax.fori_loop(1, count, step, 0)

    def greet(device, _):
        pl.semaphore_signal(barrier, inc=1, device_id=device, device_id_type=MESH)

    others("freq", nq, q, greet)
    others("space", ne, e, greet)
    pl.semaphore_wait(barrier, nq + ne - 2)

    def exchange(slot, axis, count, index, source, target):
        def act(device, i):
            pltpu.make_async_remote_copy(
                src_ref=source(i), dst_ref=target.at[index],
                send_sem=send_sem.at[slot], recv_sem=recv_sem.at[slot],
                device_id=device, device_id_type=MESH,
            ).start()

        pltpu.make_async_copy(source(index), target.at[index], recv_sem.at[slot]).start()
        others(axis, count, index, act)

        def finish():
            pltpu.make_async_copy(target, target, recv_sem.at[slot]).wait()
            rest = target.at[pl.ds(0, count - 1)]
            pltpu.make_async_copy(rest, rest, send_sem.at[slot]).wait()

        return finish

    got_spec = exchange(0, "freq", nq, q, lambda i: spec_ref.at[i], spec_all)
    got_sums = exchange(1, "freq", nq, q, lambda i: own_ref.at[i], sums_ref)

    got_spec()

    def widen(b, carry):
        block = spec_all[b].astype(jnp.float32)
        there = pl.ds(pl.multiple_of(b * pad, pad), cols)
        for h in range(width // LANES):
            flat[h, there, :] = block[:, h * LANES : (h + 1) * LANES]
        return carry

    lax.fori_loop(0, blocks, widen, 0)
    for j in range(cols):
        for h in range(width // LANES):
            rows[j * blocks : (j + 1) * blocks, h * LANES : (h + 1) * LANES] = flat[
                h, pl.ds(j, blocks, stride=pad), :
            ].astype(jnp.bfloat16)

    half = width // 2
    for c in range(triads // 256):
        lanes = slice(c * 256, (c + 1) * 256)
        at = lax.broadcasted_iota(jnp.int32, (width, 256), 0)

        def pick(row, shift):
            hot = jnp.where(at == triad_ref[row : row + 1, lanes] + shift, 1.0, 0.0)
            return hot.astype(jnp.bfloat16)

        hots = [pick(row, shift) for row in range(3) for shift in (0, half)]
        for j in range(0, cols, 2):
            here = slice(j * blocks, (j + 2) * blocks)
            k_re, k_im, l_re, l_im, s_re, s_im = [
                jnp.dot(rows[here, :], hot, preferred_element_type=jnp.float32) for hot in hots
            ]
            weight = weight_ref[here, :]
            weight = jnp.concatenate([weight, weight], axis=1)
            prod_re[here, lanes] = ((k_re * l_re - k_im * l_im) * weight).astype(jnp.bfloat16)
            prod_im[here, lanes] = ((k_re * l_im + k_im * l_re) * weight).astype(jnp.bfloat16)
            sum_re[here, lanes] = s_re.astype(jnp.bfloat16)
            sum_im[here, lanes] = s_im.astype(jnp.bfloat16)

    coef_ref[0] = jnp.ones((blocks, triads), jnp.float32)
    coef_ref[1] = jnp.zeros((blocks, triads), jnp.float32)

    for sweep in range(2):
        for g in range(groups):
            lanes = slice(g * LANES, (g + 1) * LANES)
            a_re, a_im = coef_ref[0, :, lanes], coef_ref[1, :, lanes]

            def column(j, carry):
                v_re, v_im = carry
                here = pl.ds(pl.multiple_of(j * blocks, blocks), blocks)
                s_re = sum_re[here, lanes].astype(jnp.float32)
                s_im = sum_im[here, lanes].astype(jnp.float32)
                f_re = jnp.sum(a_re * s_re - a_im * s_im, axis=0, keepdims=True)
                f_im = jnp.sum(a_re * s_im + a_im * s_re, axis=0, keepdims=True)
                p_re = prod_re[here, lanes].astype(jnp.float32)
                p_im = prod_im[here, lanes].astype(jnp.float32)
                return (v_re + (p_re * f_re + p_im * f_im), v_im + (p_re * f_im - p_im * f_re))

            zero = jnp.zeros((blocks, LANES), jnp.float32)
            v_re, v_im = lax.fori_loop(0, cols, column, (zero, zero))
            part[sweep, 0, :, lanes] = v_re
            part[sweep, 1, :, lanes] = v_im

        base = 2 + 4 * sweep
        exchange(
            base, "space", ne, e,
            lambda i: part.at[sweep, :, pl.ds(pl.multiple_of(i * per_e, per_e), per_e), :],
            part_in.at[sweep],
        )()
        total = jnp.sum(part_in[sweep], axis=0)
        for r in range(2):
            for b in range(per_e):
                for g in range(groups):
                    piece[sweep, (r * per_e + b) * groups + g] = total[
                        r, b : b + 1, g * LANES : (g + 1) * LANES
                    ]
        exchange(
            base + 1, "freq", nq, q, lambda i: piece.at[sweep, i], piece_in.at[sweep]
        )()
        mine[sweep] = jnp.sum(piece_in[sweep], axis=0)
        exchange(base + 2, "freq", nq, q, lambda i: mine.at[sweep], gathered.at[sweep])()
        exchange(base + 3, "space", ne, e, lambda i: gathered.at[sweep], spread.at[sweep])()

        def place(d, carry):
            for r in range(2):
                for g in range(groups):
                    block = jnp.concatenate(
                        [spread[sweep, d, (r * per_e + b) * groups + g] for b in range(per_e)], axis=0
                    )
                    there = pl.ds(pl.multiple_of(d * per_e, per_e), per_e)
                    coef_ref[r, there, g * LANES : (g + 1) * LANES] = block
            return carry

        lax.fori_loop(0, ne, place, 0)
        v_re, v_im = coef_ref[0], coef_ref[1]
        energy = jnp.sum(v_re * v_re + v_im * v_im, axis=0, keepdims=True) / blocks
        factor = lax.rsqrt(energy + 1e-05)
        coef_ref[0] = v_re * factor
        coef_ref[1] = v_im * factor

    got_sums()


def exchange_and_iterate(nq, ne, spec, own, weight, triad):
    blocks, cols, width = spec.shape
    triads = triad.shape[1]
    pieces = 2 * (blocks // ne) * (triads // LANES)
    assert pieces == nq
    f32, bf16 = jnp.float32, jnp.bfloat16
    vmem = pl.BlockSpec(memory_space=pltpu.VMEM)
    return pl.pallas_call(
        functools.partial(kernel, nq, ne),
        out_shape=(
            jax.ShapeDtypeStruct((2, blocks, triads), f32),
            jax.ShapeDtypeStruct(own.shape, bf16),
        ),
        in_specs=[vmem] * 4,
        out_specs=(vmem, vmem),
        scratch_shapes=[
            pltpu.VMEM((blocks, cols, width), bf16),
            pltpu.VMEM((width // LANES, blocks * 16, LANES), f32),
            pltpu.VMEM((cols * blocks, width), bf16),
            pltpu.VMEM((cols * blocks, triads), bf16),
            pltpu.VMEM((cols * blocks, triads), bf16),
            pltpu.VMEM((cols * blocks, triads), bf16),
            pltpu.VMEM((cols * blocks, triads), bf16),
            pltpu.VMEM((8, LANES), f32),
            pltpu.VMEM((2, 2, blocks, triads), f32),
            pltpu.VMEM((2, ne, 2, blocks // ne, triads), f32),
            pltpu.VMEM((2, pieces, 1, LANES), f32),
            pltpu.VMEM((2, nq, 1, LANES), f32),
            pltpu.VMEM((2, 1, LANES), f32),
            pltpu.VMEM((2, nq, 1, LANES), f32),
            pltpu.VMEM((2, ne, nq, 1, LANES), f32),
            pltpu.SemaphoreType.DMA((10,)),
            pltpu.SemaphoreType.DMA((10,)),
        ],
        compiler_params=pltpu.CompilerParams(
            collective_id=0, has_side_effects=True, vmem_limit_bytes=48 * 1024 * 1024
        ),
    )(spec, own, weight, triad)


def body(snapshots, point_weights, owner_map, triad_list):
    samples = snapshots.shape[1]
    points = snapshots.shape[3]
    columns = 3 * points
    frequencies = owner_map.shape[0]
    triad_count = triad_list.shape[0]
    nq, ne = lax.axis_size("freq"), lax.axis_size("space")
    triads_here = triad_count // nq
    slots = frequencies // nq
    per_slot = triads_here // slots
    mine = lax.axis_index("freq")
    table = make_table(samples, frequencies)
    data = snapshots.reshape(samples, columns)
    by_part = table.reshape(frequencies, 2, samples).transpose(1, 0, 2).reshape(2 * frequencies, samples)
    spec = lax.dot_general(
        data, by_part, (((0,), (1,)), ((), ())), preferred_element_type=jnp.float32
    ).astype(jnp.bfloat16)
    owned_table = select_rows(owner_map, table.reshape(frequencies, 2 * samples))
    own = jnp.dot(
        owned_table.astype(jnp.bfloat16).reshape(2 * frequencies, samples),
        data,
        preferred_element_type=jnp.float32,
    ).astype(jnp.bfloat16)
    cols = columns // nq
    weight = lax.dynamic_slice(jnp.tile(point_weights, 3), (mine * cols,), (cols,))
    weight = jnp.broadcast_to(weight[:, None, None], (cols, nq, LANES)).reshape(cols * nq, LANES)
    first, second = triad_list[:, 0], triad_list[:, 1]
    triad = jnp.stack([first, second, first + second])
    coef, sums = exchange_and_iterate(
        nq, ne, spec.reshape(nq, cols, 2 * frequencies), own.reshape(nq, 2 * slots, columns), weight, triad
    )
    coefficients = lax.dynamic_slice(coef, (0, 0, mine * triads_here), (2, nq, triads_here))
    coefficients = coefficients.transpose(2, 0, 1)
    sums = sums.reshape(nq, slots, 2, columns)
    sums_f = sums.astype(jnp.float32)
    power_map = jnp.sum((sums_f * sums_f).reshape(nq, slots, 6, points), axis=(0, 2)) / nq
    rounded = coefficients.astype(jnp.bfloat16).reshape(per_slot, slots, 2, nq)
    out = jnp.einsum("quxb,buyk->quxyk", rounded, sums, preferred_element_type=jnp.float32)
    mode_real = out[:, :, 0, 0] - out[:, :, 1, 1]
    mode_imag = out[:, :, 0, 1] + out[:, :, 1, 0]
    modes = jnp.stack([mode_real, mode_imag], axis=2) / math.sqrt(nq)
    return (power_map, coefficients, modes.reshape(triads_here, 2, 3, points))


def solution(mesh):
    placed = (P("freq", None, None, "space"), P("space"), P(), P())
    return jax.shard_map(
        body,
        mesh=mesh,
        in_specs=placed,
        out_specs=(P("freq", "space"), P("freq", None, None), P("freq", None, None, "space")),
        check_vma=False,
    )
```

```python
import functools
import math

import jax
import jax.numpy as jnp
from jax import lax
from jax.experimental import pallas as pl
from jax.experimental.pallas import tpu as pltpu
from jax.sharding import PartitionSpec as P


def make_table(samples, frequencies):
    sample_idx = jnp.arange(samples, dtype=jnp.int32)
    freq_idx = jnp.arange(frequencies, dtype=jnp.int32)
    angles = (freq_idx[:, None] * sample_idx[None, :] % samples).astype(jnp.float32) * (
        2.0 * math.pi / samples
    )
    window = 0.5 - 0.5 * jnp.cos(sample_idx.astype(jnp.float32) * (2.0 * math.pi / samples))
    taper = window / math.sqrt(samples)
    stacked = jnp.stack([jnp.cos(angles) * taper, -jnp.sin(angles) * taper], axis=1)
    return stacked.reshape(2 * frequencies, samples).astype(jnp.bfloat16)


def select_rows(index, rows):
    hot = (index[:, None] == jnp.arange(rows.shape[0], dtype=jnp.int32)[None, :]).astype(jnp.bfloat16)
    return jnp.dot(hot, rows, preferred_element_type=jnp.float32)


def normalized(vec_real, vec_imag):
    energy = jnp.mean(vec_real * vec_real + vec_imag * vec_imag, axis=-1, keepdims=True)
    factor = lax.rsqrt(energy + 1e-05)
    return (vec_real * factor, vec_imag * factor)


MESH = pl.DeviceIdType.MESH
LANES = 128


def kernel(
    nq, ne, spec_ref, own_ref, weight_ref, triad_ref,
    last_ref, sums_ref,
    spec_all, flat, rows, prod_re, prod_im, sum_re, sum_im, field,
    coef_ref, part, part_in, piece, piece_in, mine, gathered, spread,
    send_sem, recv_sem,
):
    q = lax.axis_index("freq")
    e = lax.axis_index("space")
    blocks, bands, band, width = spec_ref.shape
    cols = bands * band
    pad = flat.shape[1] // blocks
    triads = triad_ref.shape[1]
    per_e = blocks // ne
    groups = triads // LANES

    barrier = pltpu.get_barrier_semaphore()

    def others(axis, count, index, act):
        def step(i, carry):
            act({axis: lax.rem(index + i, count)}, lax.rem(index + i, count))
            return carry

        lax.fori_loop(1, count, step, 0)

    def greet(device, _):
        pl.semaphore_signal(barrier, inc=1, device_id=device, device_id_type=MESH)

    others("freq", nq, q, greet)
    others("space", ne, e, greet)
    pl.semaphore_wait(barrier, nq + ne - 2)

    def exchange(slot, axis, count, index, source, target):
        def act(device, i):
            pltpu.make_async_remote_copy(
                src_ref=source(i), dst_ref=target.at[index],
                send_sem=send_sem.at[slot], recv_sem=recv_sem.at[slot],
                device_id=device, device_id_type=MESH,
            ).start()

        pltpu.make_async_copy(source(index), target.at[index], recv_sem.at[slot]).start()
        others(axis, count, index, act)

        def finish():
            pltpu.make_async_copy(target, target, recv_sem.at[slot]).wait()
            rest = target.at[pl.ds(0, count - 1)]
            pltpu.make_async_copy(rest, rest, send_sem.at[slot]).wait()

        return finish

    got_spec = exchange(0, "freq", nq, q, lambda i: spec_ref.at[i], spec_all)
    got_spec()

    def widen(b, carry):
        for k in range(bands):
            block = spec_all[b, k].astype(jnp.float32)
            there = pl.ds(b * pad + k * band, band)
            for h in range(width // LANES):
                flat[h, there, :] = block[:, h * LANES : (h + 1) * LANES]
        return carry

    lax.fori_loop(0, blocks, widen, 0)
    for j in range(cols):
        for h in range(width // LANES):
            rows[j * blocks : (j + 1) * blocks, h * LANES : (h + 1) * LANES] = flat[
                h, pl.ds(j, blocks, stride=pad), :
            ].astype(jnp.bfloat16)

    half = width // 2
    for c in range(triads // 256):
        lanes = slice(c * 256, (c + 1) * 256)
        at = lax.broadcasted_iota(jnp.int32, (width, 256), 0)

        def pick(row, shift):
            hot = jnp.where(at == triad_ref[row : row + 1, lanes] + shift, 1.0, 0.0)
            return hot.astype(jnp.bfloat16)

        hots = [pick(row, shift) for row in range(3) for shift in (0, half)]
        for j in range(0, cols, 2):
            here = slice(j * blocks, (j + 2) * blocks)
            k_re, k_im, l_re, l_im, s_re, s_im = [
                jnp.dot(rows[here, :], hot, preferred_element_type=jnp.float32) for hot in hots
            ]
            weight = weight_ref[here, :]
            weight = jnp.concatenate([weight, weight], axis=1)
            prod_re[here, lanes] = ((k_re * l_re - k_im * l_im) * weight).astype(jnp.bfloat16)
            prod_im[here, lanes] = ((k_re * l_im + k_im * l_re) * weight).astype(jnp.bfloat16)
            sum_re[here, lanes] = s_re.astype(jnp.bfloat16)
            sum_im[here, lanes] = s_im.astype(jnp.bfloat16)

    coef_ref[0] = jnp.ones((blocks, triads), jnp.float32)
    coef_ref[1] = jnp.zeros((blocks, triads), jnp.float32)

    for sweep in range(2):
        for g in range(groups):
            lanes = slice(g * LANES, (g + 1) * LANES)
            a_re, a_im = coef_ref[0, :, lanes], coef_ref[1, :, lanes]

            def column(j, carry):
                v_re, v_im = carry
                here = pl.ds(pl.multiple_of(j * blocks, blocks), blocks)
                s_re = sum_re[here, lanes].astype(jnp.float32)
                s_im = sum_im[here, lanes].astype(jnp.float32)
                f_re = jnp.sum(a_re * s_re - a_im * s_im, axis=0, keepdims=True)
                f_im = jnp.sum(a_re * s_im + a_im * s_re, axis=0, keepdims=True)
                p_re = prod_re[here, lanes].astype(jnp.float32)
                p_im = prod_im[here, lanes].astype(jnp.float32)
                return (v_re + (p_re * f_re + p_im * f_im), v_im + (p_re * f_im - p_im * f_re))

            zero = jnp.zeros((blocks, LANES), jnp.float32)
            v_re, v_im = lax.fori_loop(0, cols, column, (zero, zero))
            part[sweep, 0, :, lanes] = v_re
            part[sweep, 1, :, lanes] = v_im

        base = 2 + 4 * sweep
        exchange(
            base, "space", ne, e,
            lambda i: part.at[sweep, :, pl.ds(pl.multiple_of(i * per_e, per_e), per_e), :],
            part_in.at[sweep],
        )()
        total = jnp.sum(part_in[sweep], axis=0)
        if sweep == 0:
            for r in range(2):
                for b in range(per_e):
                    for g in range(groups):
                        piece[sweep, (r * per_e + b) * groups + g] = total[
                            r, b : b + 1, g * LANES : (g + 1) * LANES
                        ]
        else:
            stack = jnp.concatenate(
                [total[r, :, g * LANES : (g + 1) * LANES] for g in range(groups) for r in range(2)], axis=0
            )
            blank = jnp.zeros_like(stack)
            even = jnp.concatenate([stack, blank], axis=0).T
            odd = jnp.concatenate([blank, stack], axis=0).T
            by_owner = even[:nq] + odd[nq:]
            for i in range(nq):
                piece[sweep, i] = by_owner[i : i + 1]
        exchange(
            base + 1, "freq", nq, q, lambda i: piece.at[sweep, i], piece_in.at[sweep]
        )()
        mine[sweep] = jnp.sum(piece_in[sweep], axis=0)
        if sweep == 1:
            exchange(base + 3, "space", ne, e, lambda i: mine.at[sweep], last_ref)()
            break
        got_mine = exchange(base + 2, "freq", nq, q, lambda i: mine.at[sweep], gathered)
        got_sums = exchange(1, "freq", nq, q, lambda i: own_ref.at[i], sums_ref)
        got_mine()
        exchange(base + 3, "space", ne, e, lambda i: gathered, spread)()

        def place(d, carry):
            for r in range(2):
                for g in range(groups):
                    block = jnp.concatenate(
                        [spread[d, (r * per_e + b) * groups + g] for b in range(per_e)], axis=0
                    )
                    there = pl.ds(pl.multiple_of(d * per_e, per_e), per_e)
                    coef_ref[r, there, g * LANES : (g + 1) * LANES] = block
            return carry

        lax.fori_loop(0, ne, place, 0)
        v_re, v_im = coef_ref[0], coef_ref[1]
        energy = jnp.sum(v_re * v_re + v_im * v_im, axis=0, keepdims=True) / blocks
        factor = lax.rsqrt(energy + 1e-05)
        coef_ref[0] = v_re * factor
        coef_ref[1] = v_im * factor

    got_sums()


def exchange_and_iterate(nq, ne, spec, own, weight, triad):
    blocks, bands, band, width = spec.shape
    cols = bands * band
    triads = triad.shape[1]
    pieces = 2 * (blocks // ne) * (triads // LANES)
    assert pieces == nq and LANES == 2 * nq and triads == 8 * nq
    f32, bf16 = jnp.float32, jnp.bfloat16
    vmem = pl.BlockSpec(memory_space=pltpu.VMEM)
    return pl.pallas_call(
        functools.partial(kernel, nq, ne),
        out_shape=(
            jax.ShapeDtypeStruct((ne, 1, LANES), f32),
            jax.ShapeDtypeStruct(own.shape, bf16),
        ),
        in_specs=[vmem] * 4,
        out_specs=(vmem, vmem),
        scratch_shapes=[
            pltpu.VMEM((blocks, bands, band, width), bf16),
            pltpu.VMEM((width // LANES, blocks * 16, LANES), f32),
            pltpu.VMEM((cols * blocks, width), bf16),
            pltpu.VMEM((cols * blocks, triads), bf16),
            pltpu.VMEM((cols * blocks, triads), bf16),
            pltpu.VMEM((cols * blocks, triads), bf16),
            pltpu.VMEM((cols * blocks, triads), bf16),
            pltpu.VMEM((8, LANES), f32),
            pltpu.VMEM((2, blocks, triads), f32),
            pltpu.VMEM((2, 2, blocks, triads), f32),
            pltpu.VMEM((2, ne, 2, blocks // ne, triads), f32),
            pltpu.VMEM((2, pieces, 1, LANES), f32),
            pltpu.VMEM((2, nq, 1, LANES), f32),
            pltpu.VMEM((2, 1, LANES), f32),
            pltpu.VMEM((nq, 1, LANES), f32),
            pltpu.VMEM((ne, nq, 1, LANES), f32),
            pltpu.SemaphoreType.DMA((10,)),
            pltpu.SemaphoreType.DMA((10,)),
        ],
        compiler_params=pltpu.CompilerParams(
            collective_id=0, has_side_effects=True, vmem_limit_bytes=48 * 1024 * 1024
        ),
    )(spec, own, weight, triad)


def body(snapshots, point_weights, owner_map, triad_list):
    samples = snapshots.shape[1]
    points = snapshots.shape[3]
    columns = 3 * points
    frequencies = owner_map.shape[0]
    triad_count = triad_list.shape[0]
    nq, ne = lax.axis_size("freq"), lax.axis_size("space")
    triads_here = triad_count // nq
    slots = frequencies // nq
    per_slot = triads_here // slots
    mine = lax.axis_index("freq")
    table = make_table(samples, frequencies)
    data = snapshots.reshape(samples, columns)
    by_part = table.reshape(frequencies, 2, samples).transpose(1, 0, 2).reshape(2 * frequencies, samples)
    spec = lax.dot_general(
        data, by_part, (((0,), (1,)), ((), ())), preferred_element_type=jnp.float32
    ).astype(jnp.bfloat16)
    owned_table = select_rows(owner_map, table.reshape(frequencies, 2 * samples))
    own = jnp.dot(
        owned_table.astype(jnp.bfloat16).reshape(2 * frequencies, samples),
        data,
        preferred_element_type=jnp.float32,
    ).astype(jnp.bfloat16)
    cols = columns // nq
    weight = lax.dynamic_slice(jnp.tile(point_weights, 3), (mine * cols,), (cols,))
    weight = jnp.broadcast_to(weight[:, None, None], (cols, nq, LANES)).reshape(cols * nq, LANES)
    first, second = triad_list[:, 0], triad_list[:, 1]
    triad = jnp.stack([first, second, first + second])
    triad = triad.reshape(3, nq, triads_here).transpose(0, 2, 1).reshape(3, triad_count)
    last, sums = exchange_and_iterate(
        nq, ne, spec.reshape(nq, cols // 4, 4, 2 * frequencies), own.reshape(nq, 2 * slots, columns), weight, triad
    )
    vec = last.reshape(ne, 2, triads_here // 2, 2, nq // ne).transpose(2, 1, 3, 0, 4)
    vec = vec.reshape(triads_here, 2, nq)
    coefficients = jnp.stack(normalized(vec[:, 0], vec[:, 1]), axis=1)
    sums = sums.reshape(nq, slots, 2, columns)
    sums_f = sums.astype(jnp.float32)
    power_map = jnp.sum((sums_f * sums_f).reshape(nq, slots, 6, points), axis=(0, 2)) / nq
    rounded = coefficients.astype(jnp.bfloat16).reshape(per_slot, slots, 2, nq)
    out = jnp.einsum("quxb,buyk->quxyk", rounded, sums, preferred_element_type=jnp.float32)
    mode_real = out[:, :, 0, 0] - out[:, :, 1, 1]
    mode_imag = out[:, :, 0, 1] + out[:, :, 1, 0]
    modes = jnp.stack([mode_real, mode_imag], axis=2) / math.sqrt(nq)
    return (power_map, coefficients, modes.reshape(triads_here, 2, 3, points))


def solution(mesh):
    placed = (P("freq", None, None, "space"), P("space"), P(), P())
    return jax.shard_map(
        body,
        mesh=mesh,
        in_specs=placed,
        out_specs=(P("freq", "space"), P("freq", None, None), P("freq", None, None, "space")),
        check_vma=False,
    )
```

```python
import functools
import math

import jax
import jax.numpy as jnp
from jax import lax
from jax.experimental import pallas as pl
from jax.experimental.pallas import tpu as pltpu
from jax.sharding import PartitionSpec as P


def make_table(samples, frequencies):
    sample_idx = jnp.arange(samples, dtype=jnp.int32)
    freq_idx = jnp.arange(frequencies, dtype=jnp.int32)
    angles = (freq_idx[:, None] * sample_idx[None, :] % samples).astype(jnp.float32) * (
        2.0 * math.pi / samples
    )
    window = 0.5 - 0.5 * jnp.cos(sample_idx.astype(jnp.float32) * (2.0 * math.pi / samples))
    taper = window / math.sqrt(samples)
    stacked = jnp.stack([jnp.cos(angles) * taper, -jnp.sin(angles) * taper], axis=1)
    return stacked.reshape(2 * frequencies, samples).astype(jnp.bfloat16)


def select_rows(index, rows):
    hot = (index[:, None] == jnp.arange(rows.shape[0], dtype=jnp.int32)[None, :]).astype(jnp.bfloat16)
    return jnp.dot(hot, rows, preferred_element_type=jnp.float32)


def normalized(vec_real, vec_imag):
    energy = jnp.mean(vec_real * vec_real + vec_imag * vec_imag, axis=-1, keepdims=True)
    factor = lax.rsqrt(energy + 1e-05)
    return (vec_real * factor, vec_imag * factor)


MESH = pl.DeviceIdType.MESH
LANES = 128


def kernel(
    nq, ne, spec_ref, own_ref, weight_ref, triad_ref,
    last_ref, sums_ref, power_ref,
    weight_rows, spec_all, flat, rows, prod_re, prod_im, sum_re, sum_im, field,
    coef_ref, part, part_in, piece, piece_in, mine, gathered, spread,
    send_sem, recv_sem,
):
    q = lax.axis_index("freq")
    e = lax.axis_index("space")
    blocks, bands, band, width = spec_ref.shape
    cols = bands * band
    pad = flat.shape[1] // blocks
    triads = triad_ref.shape[1]
    per_e = blocks // ne
    groups = triads // LANES

    barrier = pltpu.get_barrier_semaphore()

    ring = 16

    def far_first(k, count):
        return (count // 2 + (1 - 2 * (k % 2)) * ((k + 1) // 2)) % count

    def others(axis, count, index, act):
        def step(k, carry):
            if axis == "freq":
                outer = count // ring
                far_z, far_y = far_first(k // outer, ring), far_first(k % outer, outer)
                i = (index // ring + far_y) % outer * ring + (index + far_z) % ring
            else:
                i = (index + far_first(k, count)) % count
            act({axis: i}, i)
            return carry

        lax.fori_loop(0, count - 1, step, 0)

    def greet(device, _):
        pl.semaphore_signal(barrier, inc=1, device_id=device, device_id_type=MESH)

    others("freq", nq, q, greet)
    others("space", ne, e, greet)
    for j in range(cols):
        value = weight_ref[(q * cols + j) % weight_ref.shape[0]]
        weight_rows[j * blocks : (j + 1) * blocks, :] = jnp.full((blocks, LANES), value)
    pl.semaphore_wait(barrier, nq + ne - 2)

    def exchange(slot, axis, count, index, source, target):
        def act(device, i):
            pltpu.make_async_remote_copy(
                src_ref=source(i), dst_ref=target.at[index],
                send_sem=send_sem.at[slot], recv_sem=recv_sem.at[slot],
                device_id=device, device_id_type=MESH,
            ).start()

        pltpu.make_async_copy(source(index), target.at[index], recv_sem.at[slot]).start()
        others(axis, count, index, act)

        def finish():
            pltpu.make_async_copy(target, target, recv_sem.at[slot]).wait()
            rest = target.at[pl.ds(0, count - 1)]
            pltpu.make_async_copy(rest, rest, send_sem.at[slot]).wait()

        return finish

    got_spec = exchange(0, "freq", nq, q, lambda i: spec_ref.at[i], spec_all)
    got_spec()

    def widen(b, carry):
        for k in range(bands):
            block = spec_all[b, k].astype(jnp.float32)
            there = pl.ds(b * pad + k * band, band)
            for h in range(width // LANES):
                flat[h, there, :] = block[:, h * LANES : (h + 1) * LANES]
        return carry

    lax.fori_loop(0, blocks, widen, 0)
    for j in range(cols):
        for h in range(width // LANES):
            rows[j * blocks : (j + 1) * blocks, h * LANES : (h + 1) * LANES] = flat[
                h, pl.ds(j, blocks, stride=pad), :
            ].astype(jnp.bfloat16)

    half = width // 2
    for c in range(triads // 256):
        lanes = slice(c * 256, (c + 1) * 256)
        at = lax.broadcasted_iota(jnp.int32, (width, 256), 0)

        def pick(row, shift):
            hot = jnp.where(at == triad_ref[row : row + 1, lanes] + shift, 1.0, 0.0)
            return hot.astype(jnp.bfloat16)

        hots = [pick(row, shift) for row in range(3) for shift in (0, half)]
        for j in range(0, cols, 2):
            here = slice(j * blocks, (j + 2) * blocks)
            k_re, k_im, l_re, l_im, s_re, s_im = [
                jnp.dot(rows[here, :], hot, preferred_element_type=jnp.float32) for hot in hots
            ]
            weight = weight_rows[here, :]
            weight = jnp.concatenate([weight, weight], axis=1)
            prod_re[here, lanes] = ((k_re * l_re - k_im * l_im) * weight).astype(jnp.bfloat16)
            prod_im[here, lanes] = ((k_re * l_im + k_im * l_re) * weight).astype(jnp.bfloat16)
            sum_re[here, lanes] = s_re.astype(jnp.bfloat16)
            sum_im[here, lanes] = s_im.astype(jnp.bfloat16)

    coef_ref[0] = jnp.ones((blocks, triads), jnp.float32)
    coef_ref[1] = jnp.zeros((blocks, triads), jnp.float32)

    for sweep in range(2):
        for g in range(groups):
            lanes = slice(g * LANES, (g + 1) * LANES)
            a_re, a_im = coef_ref[0, :, lanes], coef_ref[1, :, lanes]

            def column(j, carry):
                v_re, v_im = carry
                here = pl.ds(pl.multiple_of(j * blocks, blocks), blocks)
                s_re = sum_re[here, lanes].astype(jnp.float32)
                s_im = sum_im[here, lanes].astype(jnp.float32)
                f_re = jnp.sum(a_re * s_re - a_im * s_im, axis=0, keepdims=True)
                f_im = jnp.sum(a_re * s_im + a_im * s_re, axis=0, keepdims=True)
                p_re = prod_re[here, lanes].astype(jnp.float32)
                p_im = prod_im[here, lanes].astype(jnp.float32)
                return (v_re + (p_re * f_re + p_im * f_im), v_im + (p_re * f_im - p_im * f_re))

            zero = jnp.zeros((blocks, LANES), jnp.float32)
            v_re, v_im = lax.fori_loop(0, cols, column, (zero, zero))
            part[sweep, 0, :, lanes] = v_re
            part[sweep, 1, :, lanes] = v_im

        base = 2 + 4 * sweep
        exchange(
            base, "space", ne, e,
            lambda i: part.at[sweep, :, pl.ds(pl.multiple_of(i * per_e, per_e), per_e), :],
            part_in.at[sweep],
        )()
        total = jnp.sum(part_in[sweep], axis=0)
        if sweep == 0:
            for r in range(2):
                for b in range(per_e):
                    for g in range(groups):
                        piece[sweep, (r * per_e + b) * groups + g] = total[
                            r, b : b + 1, g * LANES : (g + 1) * LANES
                        ]
        else:
            stack = jnp.concatenate(
                [total[r, :, g * LANES : (g + 1) * LANES] for g in range(groups) for r in range(2)], axis=0
            )
            blank = jnp.zeros_like(stack)
            even = jnp.concatenate([stack, blank], axis=0).T
            odd = jnp.concatenate([blank, stack], axis=0).T
            by_owner = even[:nq] + odd[nq:]
            for i in range(nq):
                piece[sweep, i] = by_owner[i : i + 1]
        got_piece = exchange(
            base + 1, "freq", nq, q, lambda i: piece.at[sweep, i], piece_in.at[sweep]
        )
        if sweep == 1:
            got_sums()

            def energy_of(b, total):
                values = sums_ref[b].astype(jnp.float32)
                return total + values * values

            energy = lax.fori_loop(0, blocks, energy_of, jnp.zeros(sums_ref.shape[1:], jnp.float32))
            points = power_ref.shape[1]
            for slot in range(power_ref.shape[0]):
                pair = energy[2 * slot : 2 * slot + 1] + energy[2 * slot + 1 : 2 * slot + 2]
                pair = pair[:, :points] + pair[:, points : 2 * points] + pair[:, 2 * points :]
                power_ref[slot : slot + 1, :] = pair / blocks
        got_piece()
        mine[sweep] = jnp.sum(piece_in[sweep], axis=0)
        if sweep == 1:
            exchange(base + 3, "space", ne, e, lambda i: mine.at[sweep], last_ref)()
            break
        got_mine = exchange(base + 2, "freq", nq, q, lambda i: mine.at[sweep], gathered)
        got_sums = exchange(1, "freq", nq, q, lambda i: own_ref.at[i], sums_ref)
        got_mine()
        exchange(base + 3, "space", ne, e, lambda i: gathered, spread)()

        def place(d, carry):
            for r in range(2):
                for g in range(groups):
                    block = jnp.concatenate(
                        [spread[d, (r * per_e + b) * groups + g] for b in range(per_e)], axis=0
                    )
                    there = pl.ds(pl.multiple_of(d * per_e, per_e), per_e)
                    coef_ref[r, there, g * LANES : (g + 1) * LANES] = block
            return carry

        lax.fori_loop(0, ne, place, 0)
        v_re, v_im = coef_ref[0], coef_ref[1]
        energy = jnp.sum(v_re * v_re + v_im * v_im, axis=0, keepdims=True) / blocks
        factor = lax.rsqrt(energy + 1e-05)
        coef_ref[0] = v_re * factor
        coef_ref[1] = v_im * factor


def exchange_and_iterate(nq, ne, spec, own, weight, triad):
    blocks, bands, band, width = spec.shape
    cols = bands * band
    triads = triad.shape[1]
    pieces = 2 * (blocks // ne) * (triads // LANES)
    assert pieces == nq and LANES == 2 * nq and triads == 8 * nq
    f32, bf16 = jnp.float32, jnp.bfloat16
    vmem = pl.BlockSpec(memory_space=pltpu.VMEM)
    return pl.pallas_call(
        functools.partial(kernel, nq, ne),
        out_shape=(
            jax.ShapeDtypeStruct((ne, 1, LANES), f32),
            jax.ShapeDtypeStruct(own.shape, bf16),
            jax.ShapeDtypeStruct((own.shape[1] // 2, own.shape[2] // 3), f32),
        ),
        in_specs=[vmem, vmem, pl.BlockSpec(memory_space=pltpu.SMEM), vmem],
        out_specs=(vmem, vmem, vmem),
        scratch_shapes=[
            pltpu.VMEM((cols * blocks, LANES), f32),
            pltpu.VMEM((blocks, bands, band, width), bf16),
            pltpu.VMEM((width // LANES, blocks * 16, LANES), f32),
            pltpu.VMEM((cols * blocks, width), bf16),
            pltpu.VMEM((cols * blocks, triads), bf16),
            pltpu.VMEM((cols * blocks, triads), bf16),
            pltpu.VMEM((cols * blocks, triads), bf16),
            pltpu.VMEM((cols * blocks, triads), bf16),
            pltpu.VMEM((8, LANES), f32),
            pltpu.VMEM((2, blocks, triads), f32),
            pltpu.VMEM((2, 2, blocks, triads), f32),
            pltpu.VMEM((2, ne, 2, blocks // ne, triads), f32),
            pltpu.VMEM((2, pieces, 1, LANES), f32),
            pltpu.VMEM((2, nq, 1, LANES), f32),
            pltpu.VMEM((2, 1, LANES), f32),
            pltpu.VMEM((nq, 1, LANES), f32),
            pltpu.VMEM((ne, nq, 1, LANES), f32),
            pltpu.SemaphoreType.DMA((10,)),
            pltpu.SemaphoreType.DMA((10,)),
        ],
        compiler_params=pltpu.CompilerParams(
            collective_id=0, has_side_effects=True, vmem_limit_bytes=48 * 1024 * 1024
        ),
    )(spec, own, weight, triad)


def body(snapshots, point_weights, owner_map, triad_list):
    samples = snapshots.shape[1]
    points = snapshots.shape[3]
    columns = 3 * points
    frequencies = owner_map.shape[0]
    triad_count = triad_list.shape[0]
    nq, ne = lax.axis_size("freq"), lax.axis_size("space")
    triads_here = triad_count // nq
    slots = frequencies // nq
    per_slot = triads_here // slots
    mine = lax.axis_index("freq")
    table = make_table(samples, frequencies)
    data = snapshots.reshape(samples, columns)
    by_part = table.reshape(frequencies, 2, samples).transpose(1, 0, 2).reshape(2 * frequencies, samples)
    spec = lax.dot_general(
        data, by_part, (((0,), (1,)), ((), ())), preferred_element_type=jnp.float32
    ).astype(jnp.bfloat16)
    owned_table = select_rows(owner_map, table.reshape(frequencies, 2 * samples))
    own = jnp.dot(
        owned_table.astype(jnp.bfloat16).reshape(2 * frequencies, samples),
        data,
        preferred_element_type=jnp.float32,
    ).astype(jnp.bfloat16)
    cols = columns // nq
    first, second = triad_list[:, 0], triad_list[:, 1]
    triad = jnp.stack([first, second, first + second])
    triad = triad.reshape(3, nq, triads_here).transpose(0, 2, 1).reshape(3, triad_count)
    last, sums, power_map = exchange_and_iterate(
        nq, ne, spec.reshape(nq, cols // 4, 4, 2 * frequencies), own.reshape(nq, 2 * slots, columns), point_weights, triad
    )
    vec = last.reshape(ne, 2, triads_here // 2, 2, nq // ne).transpose(2, 1, 3, 0, 4)
    vec = vec.reshape(triads_here, 2, nq)
    coefficients = jnp.stack(normalized(vec[:, 0], vec[:, 1]), axis=1)
    sums = sums.reshape(nq, slots, 2, columns)
    rounded = coefficients.astype(jnp.bfloat16).reshape(per_slot, slots, 2, nq)
    out = jnp.einsum("quxb,buyk->quxyk", rounded, sums, preferred_element_type=jnp.float32)
    mode_real = out[:, :, 0, 0] - out[:, :, 1, 1]
    mode_imag = out[:, :, 0, 1] + out[:, :, 1, 0]
    modes = jnp.stack([mode_real, mode_imag], axis=2) / math.sqrt(nq)
    return (power_map, coefficients, modes.reshape(triads_here, 2, 3, points))


def solution(mesh):
    placed = (P("freq", None, None, "space"), P("space"), P(), P())
    return jax.shard_map(
        body,
        mesh=mesh,
        in_specs=placed,
        out_specs=(P("freq", "space"), P("freq", None, None), P("freq", None, None, "space")),
        check_vma=False,
    )
```

```python
import functools
import math

import jax
import jax.numpy as jnp
from jax import lax
from jax.experimental import pallas as pl
from jax.experimental.pallas import tpu as pltpu
from jax.sharding import PartitionSpec as P


def make_table(samples, frequencies):
    sample_idx = jnp.arange(samples, dtype=jnp.int32)
    freq_idx = jnp.arange(frequencies, dtype=jnp.int32)
    angles = (freq_idx[:, None] * sample_idx[None, :] % samples).astype(jnp.float32) * (
        2.0 * math.pi / samples
    )
    window = 0.5 - 0.5 * jnp.cos(sample_idx.astype(jnp.float32) * (2.0 * math.pi / samples))
    taper = window / math.sqrt(samples)
    stacked = jnp.stack([jnp.cos(angles) * taper, -jnp.sin(angles) * taper], axis=1)
    return stacked.reshape(2 * frequencies, samples).astype(jnp.bfloat16)


def select_rows(index, rows):
    hot = (index[:, None] == jnp.arange(rows.shape[0], dtype=jnp.int32)[None, :]).astype(jnp.bfloat16)
    return jnp.dot(hot, rows, preferred_element_type=jnp.float32)


MESH = pl.DeviceIdType.MESH
LANES = 128


def kernel(
    nq, ne, spec_ref, own_ref, weight_ref, triad_ref,
    last_ref, sums_ref, power_ref,
    weight_rows, spec_all, flat, rows, prod_re, prod_im, sum_re, sum_im, field,
    coef_ref, part, part_in, piece, piece_in, mine, gathered, spread,
    near_sem, send_sem, recv_sem,
):
    q = lax.axis_index("freq")
    e = lax.axis_index("space")
    blocks, bands, band, width = spec_ref.shape
    cols = bands * band
    pad = flat.shape[1] // blocks
    triads = triad_ref.shape[1]
    per_e = blocks // ne
    groups = triads // LANES

    barrier = pltpu.get_barrier_semaphore()

    ring = 16

    def far_first(k, count):
        return (count // 2 + (1 - 2 * (k % 2)) * ((k + 1) // 2)) % count

    def others(axis, count, index, act):
        def step(k, carry):
            if axis == "freq":
                outer = count // ring
                far_z, far_y = far_first(k // outer, ring), far_first(k % outer, outer)
                i = (index // ring + far_y) % outer * ring + (index + far_z) % ring
            else:
                i = (index + far_first(k, count)) % count
            act({axis: i}, i)
            return carry

        lax.fori_loop(0, count - 1, step, 0)

    def row(far_y, far_z):
        rows_y = nq // ring
        return {"freq": (q // ring + far_y) % rows_y * ring + (q % ring + far_z) % ring}

    def greet(device, _):
        pl.semaphore_signal(barrier, inc=1, device_id=device, device_id_type=MESH)

    others("space", ne, e, greet)
    for far_y in range(1, nq // ring):
        greet(row(far_y, 0), None)
    for far_z in (1, ring - 1):
        greet(row(0, far_z), None)
    for j in range(cols):
        value = weight_ref[(q * cols + j) % weight_ref.shape[0]]
        weight_rows[j * blocks : (j + 1) * blocks, :] = jnp.full((blocks, LANES), value)
    pl.semaphore_wait(barrier, ne - 1 + nq // ring - 1 + 2)
    for k, far_z in enumerate((1, 1, 2, 4)):
        for other in (far_z, ring - far_z):
            pl.semaphore_signal(near_sem.at[k], inc=1, device_id=row(0, other), device_id_type=MESH)
        pl.semaphore_wait(near_sem.at[k], 2)

    def exchange(slot, axis, count, index, source, target):
        def act(device, i):
            pltpu.make_async_remote_copy(
                src_ref=source(i), dst_ref=target.at[index],
                send_sem=send_sem.at[slot], recv_sem=recv_sem.at[slot],
                device_id=device, device_id_type=MESH,
            ).start()

        pltpu.make_async_copy(source(index), target.at[index], recv_sem.at[slot]).start()
        others(axis, count, index, act)

        def finish():
            pltpu.make_async_copy(target, target, recv_sem.at[slot]).wait()
            rest = target.at[pl.ds(0, count - 1)]
            pltpu.make_async_copy(rest, rest, send_sem.at[slot]).wait()

        return finish

    got_spec = exchange(0, "freq", nq, q, lambda i: spec_ref.at[i], spec_all)
    got_spec()

    def widen(b, carry):
        for k in range(bands):
            block = spec_all[b, k].astype(jnp.float32)
            there = pl.ds(b * pad + k * band, band)
            for h in range(width // LANES):
                flat[h, there, :] = block[:, h * LANES : (h + 1) * LANES]
        return carry

    lax.fori_loop(0, blocks, widen, 0)
    for j in range(cols):
        for h in range(width // LANES):
            rows[j * blocks : (j + 1) * blocks, h * LANES : (h + 1) * LANES] = flat[
                h, pl.ds(j, blocks, stride=pad), :
            ].astype(jnp.bfloat16)

    half = width // 2
    for c in range(triads // 256):
        lanes = slice(c * 256, (c + 1) * 256)
        at = lax.broadcasted_iota(jnp.int32, (width, 256), 0)

        def pick(row, shift):
            hot = jnp.where(at == triad_ref[row : row + 1, lanes] + shift, 1.0, 0.0)
            return hot.astype(jnp.bfloat16)

        hots = [pick(row, shift) for row in range(3) for shift in (0, half)]
        for j in range(0, cols, 2):
            here = slice(j * blocks, (j + 2) * blocks)
            k_re, k_im, l_re, l_im, s_re, s_im = [
                jnp.dot(rows[here, :], hot, preferred_element_type=jnp.float32) for hot in hots
            ]
            weight = weight_rows[here, :]
            weight = jnp.concatenate([weight, weight], axis=1)
            prod_re[here, lanes] = ((k_re * l_re - k_im * l_im) * weight).astype(jnp.bfloat16)
            prod_im[here, lanes] = ((k_re * l_im + k_im * l_re) * weight).astype(jnp.bfloat16)
            sum_re[here, lanes] = s_re.astype(jnp.bfloat16)
            sum_im[here, lanes] = s_im.astype(jnp.bfloat16)

    coef_ref[0] = jnp.ones((blocks, triads), jnp.float32)
    coef_ref[1] = jnp.zeros((blocks, triads), jnp.float32)

    for sweep in range(2):
        base = 2 + 7 * sweep
        got_parts = []
        for g in range(groups):
            lanes = slice(g * LANES, (g + 1) * LANES)
            a_re, a_im = coef_ref[0, :, lanes], coef_ref[1, :, lanes]

            def column(j, carry):
                v_re, v_im = carry
                here = pl.ds(pl.multiple_of(j * blocks, blocks), blocks)
                s_re = sum_re[here, lanes].astype(jnp.float32)
                s_im = sum_im[here, lanes].astype(jnp.float32)
                f_re = jnp.sum(a_re * s_re - a_im * s_im, axis=0, keepdims=True)
                f_im = jnp.sum(a_re * s_im + a_im * s_re, axis=0, keepdims=True)
                p_re = prod_re[here, lanes].astype(jnp.float32)
                p_im = prod_im[here, lanes].astype(jnp.float32)
                return (v_re + (p_re * f_re + p_im * f_im), v_im + (p_re * f_im - p_im * f_re))

            zero = jnp.zeros((blocks, LANES), jnp.float32)
            v_re, v_im = lax.fori_loop(0, cols, column, (zero, zero))
            part[sweep, g, 0] = v_re
            part[sweep, g, 1] = v_im
            got_parts.append(
                exchange(
                    base + g, "space", ne, e,
                    lambda i: part.at[sweep, g, :, pl.ds(pl.multiple_of(i * per_e, per_e), per_e), :],
                    part_in.at[sweep, g],
                )
            )

        for got_part in got_parts:
            got_part()
        totals = [jnp.sum(part_in[sweep, g], axis=0) for g in range(groups)]
        if sweep == 0:
            for r in range(2):
                for b in range(per_e):
                    for g in range(groups):
                        piece[sweep, (r * per_e + b) * groups + g] = totals[g][
                            r, b : b + 1
                        ]
        else:
            stack = jnp.concatenate(
                [totals[g][r] for g in range(groups) for r in range(2)], axis=0
            )
            blank = jnp.zeros_like(stack)
            even = jnp.concatenate([stack, blank], axis=0).T
            odd = jnp.concatenate([blank, stack], axis=0).T
            by_owner = even[:nq] + odd[nq:]
            for i in range(nq):
                piece[sweep, i] = by_owner[i : i + 1]
        got_piece = exchange(
            base + 4, "freq", nq, q, lambda i: piece.at[sweep, i], piece_in.at[sweep]
        )
        if sweep == 1:
            got_sums()

            def energy_of(b, total):
                values = sums_ref[b].astype(jnp.float32)
                return total + values * values

            energy = lax.fori_loop(0, blocks, energy_of, jnp.zeros(sums_ref.shape[1:], jnp.float32))
            points = power_ref.shape[1]
            for slot in range(power_ref.shape[0]):
                pair = energy[2 * slot : 2 * slot + 1] + energy[2 * slot + 1 : 2 * slot + 2]
                pair = pair[:, :points] + pair[:, points : 2 * points] + pair[:, 2 * points :]
                power_ref[slot : slot + 1, :] = pair / blocks
        got_piece()
        mine[sweep] = jnp.sum(piece_in[sweep], axis=0)
        if sweep == 1:
            exchange(base + 6, "space", ne, e, lambda i: mine.at[sweep], last_ref)()
            values = jnp.concatenate([last_ref[i] for i in range(ne)], axis=0)
            square = jnp.sum(values * values, axis=0, keepdims=True)
            share = 2 * per_e
            here = lax.broadcasted_iota(jnp.int32, (LANES, LANES), 0) // share
            there = lax.broadcasted_iota(jnp.int32, (LANES, LANES), 1) // share
            same = jnp.where(here == there, 1.0, 0.0)
            energy = jnp.dot(
                jnp.broadcast_to(square, (ne, LANES)), same,
                precision=lax.Precision.HIGHEST, preferred_element_type=jnp.float32,
            )
            values = values * lax.rsqrt(energy / blocks + 1e-05)
            for i in range(ne):
                last_ref[i] = values[i : i + 1]
            break
        got_mine = exchange(base + 5, "freq", nq, q, lambda i: mine.at[sweep], gathered)
        got_sums = exchange(1, "freq", nq, q, lambda i: own_ref.at[i], sums_ref)
        got_mine()
        exchange(base + 6, "space", ne, e, lambda i: gathered, spread)()

        def place(d, carry):
            for r in range(2):
                for g in range(groups):
                    block = jnp.concatenate(
                        [spread[d, (r * per_e + b) * groups + g] for b in range(per_e)], axis=0
                    )
                    there = pl.ds(pl.multiple_of(d * per_e, per_e), per_e)
                    coef_ref[r, there, g * LANES : (g + 1) * LANES] = block
            return carry

        lax.fori_loop(0, ne, place, 0)
        v_re, v_im = coef_ref[0], coef_ref[1]
        energy = jnp.sum(v_re * v_re + v_im * v_im, axis=0, keepdims=True) / blocks
        factor = lax.rsqrt(energy + 1e-05)
        coef_ref[0] = v_re * factor
        coef_ref[1] = v_im * factor


def exchange_and_iterate(nq, ne, spec, own, weight, triad):
    blocks, bands, band, width = spec.shape
    cols = bands * band
    triads = triad.shape[1]
    pieces = 2 * (blocks // ne) * (triads // LANES)
    assert pieces == nq and LANES == 2 * nq and triads == 8 * nq
    f32, bf16 = jnp.float32, jnp.bfloat16
    vmem = pl.BlockSpec(memory_space=pltpu.VMEM)
    return pl.pallas_call(
        functools.partial(kernel, nq, ne),
        out_shape=(
            jax.ShapeDtypeStruct((ne, 1, LANES), f32),
            jax.ShapeDtypeStruct(own.shape, bf16),
            jax.ShapeDtypeStruct((own.shape[1] // 2, own.shape[2] // 3), f32),
        ),
        in_specs=[vmem, vmem, pl.BlockSpec(memory_space=pltpu.SMEM), vmem],
        out_specs=(vmem, vmem, vmem),
        scratch_shapes=[
            pltpu.VMEM((cols * blocks, LANES), f32),
            pltpu.VMEM((blocks, bands, band, width), bf16),
            pltpu.VMEM((width // LANES, blocks * 16, LANES), f32),
            pltpu.VMEM((cols * blocks, width), bf16),
            pltpu.VMEM((cols * blocks, triads), bf16),
            pltpu.VMEM((cols * blocks, triads), bf16),
            pltpu.VMEM((cols * blocks, triads), bf16),
            pltpu.VMEM((cols * blocks, triads), bf16),
            pltpu.VMEM((8, LANES), f32),
            pltpu.VMEM((2, blocks, triads), f32),
            pltpu.VMEM((2, triads // LANES, 2, blocks, LANES), f32),
            pltpu.VMEM((2, triads // LANES, ne, 2, blocks // ne, LANES), f32),
            pltpu.VMEM((2, pieces, 1, LANES), f32),
            pltpu.VMEM((2, nq, 1, LANES), f32),
            pltpu.VMEM((2, 1, LANES), f32),
            pltpu.VMEM((nq, 1, LANES), f32),
            pltpu.VMEM((ne, nq, 1, LANES), f32),
            pltpu.SemaphoreType.REGULAR((4,)),
            pltpu.SemaphoreType.DMA((16,)),
            pltpu.SemaphoreType.DMA((16,)),
        ],
        compiler_params=pltpu.CompilerParams(
            collective_id=0, has_side_effects=True, vmem_limit_bytes=48 * 1024 * 1024
        ),
    )(spec, own, weight, triad)


def body(snapshots, point_weights, owner_map, triad_list):
    samples = snapshots.shape[1]
    points = snapshots.shape[3]
    columns = 3 * points
    frequencies = owner_map.shape[0]
    triad_count = triad_list.shape[0]
    nq, ne = lax.axis_size("freq"), lax.axis_size("space")
    triads_here = triad_count // nq
    slots = frequencies // nq
    per_slot = triads_here // slots
    mine = lax.axis_index("freq")
    table = make_table(samples, frequencies)
    data = snapshots.reshape(samples, columns)
    by_part = table.reshape(frequencies, 2, samples).transpose(1, 0, 2).reshape(2 * frequencies, samples)
    spec = lax.dot_general(
        data, by_part, (((0,), (1,)), ((), ())), preferred_element_type=jnp.float32
    ).astype(jnp.bfloat16)
    owned_table = select_rows(owner_map, table.reshape(frequencies, 2 * samples))
    own = jnp.dot(
        owned_table.astype(jnp.bfloat16).reshape(2 * frequencies, samples),
        data,
        preferred_element_type=jnp.float32,
    ).astype(jnp.bfloat16)
    cols = columns // nq
    first, second = triad_list[:, 0], triad_list[:, 1]
    triad = jnp.stack([first, second, first + second])
    triad = triad.reshape(3, nq, triads_here).transpose(0, 2, 1).reshape(3, triad_count)
    last, sums, power_map = exchange_and_iterate(
        nq, ne, spec.reshape(nq, cols // 4, 4, 2 * frequencies), own.reshape(nq, 2 * slots, columns), point_weights, triad
    )
    vec = last.reshape(ne, 2, triads_here // 2, 2, nq // ne).transpose(2, 1, 3, 0, 4)
    coefficients = vec.reshape(triads_here, 2, nq)
    sums = sums.reshape(nq, slots, 2, columns)
    rounded = coefficients.astype(jnp.bfloat16).reshape(per_slot, slots, 2, nq)
    out = jnp.einsum("quxb,buyk->quxyk", rounded, sums, preferred_element_type=jnp.float32)
    mode_real = out[:, :, 0, 0] - out[:, :, 1, 1]
    mode_imag = out[:, :, 0, 1] + out[:, :, 1, 0]
    modes = jnp.stack([mode_real, mode_imag], axis=2) / math.sqrt(nq)
    return (power_map, coefficients, modes.reshape(triads_here, 2, 3, points))


def solution(mesh):
    placed = (P("freq", None, None, "space"), P("space"), P(), P())
    return jax.shard_map(
        body,
        mesh=mesh,
        in_specs=placed,
        out_specs=(P("freq", "space"), P("freq", None, None), P("freq", None, None, "space")),
        check_vma=False,
    )
```

```python
import functools
import math

import jax
import jax.numpy as jnp
from jax import lax
from jax.experimental import pallas as pl
from jax.experimental.pallas import tpu as pltpu
from jax.sharding import PartitionSpec as P


def make_table(samples, frequencies):
    sample_idx = jnp.arange(samples, dtype=jnp.int32)
    freq_idx = jnp.arange(frequencies, dtype=jnp.int32)
    angles = (freq_idx[:, None] * sample_idx[None, :] % samples).astype(jnp.float32) * (
        2.0 * math.pi / samples
    )
    window = 0.5 - 0.5 * jnp.cos(sample_idx.astype(jnp.float32) * (2.0 * math.pi / samples))
    taper = window / math.sqrt(samples)
    stacked = jnp.stack([jnp.cos(angles) * taper, -jnp.sin(angles) * taper], axis=1)
    return stacked.reshape(2 * frequencies, samples).astype(jnp.bfloat16)


def select_rows(index, rows):
    hot = (index[:, None] == jnp.arange(rows.shape[0], dtype=jnp.int32)[None, :]).astype(jnp.bfloat16)
    return jnp.dot(hot, rows, preferred_element_type=jnp.float32)


MESH = pl.DeviceIdType.MESH
LANES = 128


def kernel(
    nq, ne, spec_ref, own_ref, weight_ref, triad_ref,
    out_ref, sums_ref, power_ref,
    last_ref, weight_rows, spec_all, flat, rows, prod_re, prod_im, sum_re, sum_im, field,
    coef_ref, part, part_in, piece, piece_in, mine, gathered, spread,
    send_sem, recv_sem,
):
    q = lax.axis_index("freq")
    e = lax.axis_index("space")
    blocks, bands, band, width = spec_ref.shape
    cols = bands * band
    pad = flat.shape[1] // blocks
    triads = triad_ref.shape[1]
    per_e = blocks // ne
    groups = triads // LANES

    barrier = pltpu.get_barrier_semaphore()

    ring = 16

    def far_first(k, count):
        return (count // 2 + (1 - 2 * (k % 2)) * ((k + 1) // 2)) % count

    def others(axis, count, index, act):
        def step(k, carry):
            if axis == "freq":
                outer = count // ring
                far_z, far_y = far_first(k // outer, ring), far_first(k % outer, outer)
                i = (index // ring + far_y) % outer * ring + (index + far_z) % ring
            else:
                i = (index + far_first(k, count)) % count
            act({axis: i}, i)
            return carry

        lax.fori_loop(0, count - 1, step, 0)

    def greet(device, _):
        pl.semaphore_signal(barrier, inc=1, device_id=device, device_id_type=MESH)

    others("freq", nq, q, greet)
    others("space", ne, e, greet)
    for j in range(cols):
        value = weight_ref[(q * cols + j) % weight_ref.shape[0]]
        weight_rows[j * blocks : (j + 1) * blocks, :] = jnp.full((blocks, LANES), value)
    pl.semaphore_wait(barrier, nq + ne - 2)

    def exchange(slot, axis, count, index, source, target):
        def act(device, i):
            pltpu.make_async_remote_copy(
                src_ref=source(i), dst_ref=target.at[index],
                send_sem=send_sem.at[slot], recv_sem=recv_sem.at[slot],
                device_id=device, device_id_type=MESH,
            ).start()

        pltpu.make_async_copy(source(index), target.at[index], recv_sem.at[slot]).start()
        others(axis, count, index, act)

        def finish():
            pltpu.make_async_copy(target, target, recv_sem.at[slot]).wait()
            rest = target.at[pl.ds(0, count - 1)]
            pltpu.make_async_copy(rest, rest, send_sem.at[slot]).wait()

        return finish

    got_spec = exchange(0, "freq", nq, q, lambda i: spec_ref.at[i], spec_all)
    got_spec()

    def widen(b, carry):
        for k in range(bands):
            block = spec_all[b, k].astype(jnp.float32)
            there = pl.ds(b * pad + k * band, band)
            for h in range(width // LANES):
                flat[h, there, :] = block[:, h * LANES : (h + 1) * LANES]
        return carry

    lax.fori_loop(0, blocks, widen, 0)
    for j in range(cols):
        for h in range(width // LANES):
            rows[j * blocks : (j + 1) * blocks, h * LANES : (h + 1) * LANES] = flat[
                h, pl.ds(j, blocks, stride=pad), :
            ].astype(jnp.bfloat16)

    half = width // 2
    for c in range(triads // 256):
        lanes = slice(c * 256, (c + 1) * 256)
        at = lax.broadcasted_iota(jnp.int32, (width, 256), 0)

        def pick(row, shift):
            hot = jnp.where(at == triad_ref[row : row + 1, lanes] + shift, 1.0, 0.0)
            return hot.astype(jnp.bfloat16)

        hots = [pick(row, shift) for row in range(3) for shift in (0, half)]
        for j in range(0, cols, 2):
            here = slice(j * blocks, (j + 2) * blocks)
            k_re, k_im, l_re, l_im, s_re, s_im = [
                jnp.dot(rows[here, :], hot, preferred_element_type=jnp.float32) for hot in hots
            ]
            weight = weight_rows[here, :]
            weight = jnp.concatenate([weight, weight], axis=1)
            prod_re[here, lanes] = ((k_re * l_re - k_im * l_im) * weight).astype(jnp.bfloat16)
            prod_im[here, lanes] = ((k_re * l_im + k_im * l_re) * weight).astype(jnp.bfloat16)
            sum_re[here, lanes] = s_re.astype(jnp.bfloat16)
            sum_im[here, lanes] = s_im.astype(jnp.bfloat16)

    coef_ref[0] = jnp.ones((blocks, triads), jnp.float32)
    coef_ref[1] = jnp.zeros((blocks, triads), jnp.float32)

    for sweep in range(2):
        base = 2 + 7 * sweep
        got_parts = []
        for g in range(groups):
            lanes = slice(g * LANES, (g + 1) * LANES)
            a_re, a_im = coef_ref[0, :, lanes], coef_ref[1, :, lanes]

            def column(j, carry):
                v_re, v_im = carry
                here = pl.ds(pl.multiple_of(j * blocks, blocks), blocks)
                s_re = sum_re[here, lanes].astype(jnp.float32)
                s_im = sum_im[here, lanes].astype(jnp.float32)
                f_re = jnp.sum(a_re * s_re - a_im * s_im, axis=0, keepdims=True)
                f_im = jnp.sum(a_re * s_im + a_im * s_re, axis=0, keepdims=True)
                p_re = prod_re[here, lanes].astype(jnp.float32)
                p_im = prod_im[here, lanes].astype(jnp.float32)
                return (v_re + (p_re * f_re + p_im * f_im), v_im + (p_re * f_im - p_im * f_re))

            zero = jnp.zeros((blocks, LANES), jnp.float32)
            v_re, v_im = lax.fori_loop(0, cols, column, (zero, zero))
            part[sweep, g, 0] = v_re
            part[sweep, g, 1] = v_im
            got_parts.append(
                exchange(
                    base + g, "space", ne, e,
                    lambda i: part.at[sweep, g, :, pl.ds(pl.multiple_of(i * per_e, per_e), per_e), :],
                    part_in.at[sweep, g],
                )
            )

        for got_part in got_parts:
            got_part()
        totals = [jnp.sum(part_in[sweep, g], axis=0) for g in range(groups)]
        if sweep == 0:
            for r in range(2):
                for b in range(per_e):
                    for g in range(groups):
                        piece[sweep, (r * per_e + b) * groups + g] = totals[g][
                            r, b : b + 1
                        ]
        else:
            stack = jnp.concatenate(
                [totals[g][r] for g in range(groups) for r in range(2)], axis=0
            )
            blank = jnp.zeros_like(stack)
            even = jnp.concatenate([stack, blank], axis=0).T
            odd = jnp.concatenate([blank, stack], axis=0).T
            by_owner = even[:nq] + odd[nq:]
            for i in range(nq):
                piece[sweep, i] = by_owner[i : i + 1]
        got_piece = exchange(
            base + 4, "freq", nq, q, lambda i: piece.at[sweep, i], piece_in.at[sweep]
        )
        if sweep == 1:
            got_sums()

            def energy_of(b, total):
                values = sums_ref[b].astype(jnp.float32)
                return total + values * values

            energy = lax.fori_loop(0, blocks, energy_of, jnp.zeros(sums_ref.shape[1:], jnp.float32))
            points = power_ref.shape[1]
            for slot in range(power_ref.shape[0]):
                pair = energy[2 * slot : 2 * slot + 1] + energy[2 * slot + 1 : 2 * slot + 2]
                pair = pair[:, :points] + pair[:, points : 2 * points] + pair[:, 2 * points :]
                power_ref[slot : slot + 1, :] = pair / blocks
        got_piece()
        mine[sweep] = jnp.sum(piece_in[sweep], axis=0)
        if sweep == 1:
            exchange(base + 6, "space", ne, e, lambda i: mine.at[sweep], last_ref)()
            values = jnp.concatenate([last_ref[i] for i in range(ne)], axis=0)
            square = jnp.sum(values * values, axis=0, keepdims=True)
            share = 2 * per_e
            here = lax.broadcasted_iota(jnp.int32, (LANES, LANES), 0) // share
            there = lax.broadcasted_iota(jnp.int32, (LANES, LANES), 1) // share
            same = jnp.where(here == there, 1.0, 0.0)
            energy = jnp.dot(
                jnp.broadcast_to(square, (ne, LANES)), same,
                precision=lax.Precision.HIGHEST, preferred_element_type=jnp.float32,
            )
            values = values * lax.rsqrt(energy / blocks + 1e-05)
            lane = lax.broadcasted_iota(jnp.int32, (2 * triads // nq, LANES), 1)
            row_of = (2 * (lane // share % groups) + lane // nq) * 2 + lane // per_e % 2
            own_row = row_of == lax.broadcasted_iota(jnp.int32, row_of.shape, 0)
            wide = jnp.concatenate(
                [jnp.where(own_row, values[i : i + 1], 0.0) for i in range(ne)], axis=1
            )
            k = lax.broadcasted_iota(jnp.int32, (ne * LANES, LANES), 0)
            to = k // LANES * per_e + k % per_e
            there = jnp.where(to == lax.broadcasted_iota(jnp.int32, to.shape, 1), 1.0, 0.0)
            placed = jnp.dot(
                wide, there, precision=lax.Precision.HIGHEST, preferred_element_type=jnp.float32
            )
            out_ref[...] = placed[:, :blocks]
            break
        got_mine = exchange(base + 5, "freq", nq, q, lambda i: mine.at[sweep], gathered)
        got_sums = exchange(1, "freq", nq, q, lambda i: own_ref.at[i], sums_ref)
        got_mine()
        exchange(base + 6, "space", ne, e, lambda i: gathered, spread)()

        def place(d, carry):
            for r in range(2):
                for g in range(groups):
                    block = jnp.concatenate(
                        [spread[d, (r * per_e + b) * groups + g] for b in range(per_e)], axis=0
                    )
                    there = pl.ds(pl.multiple_of(d * per_e, per_e), per_e)
                    coef_ref[r, there, g * LANES : (g + 1) * LANES] = block
            return carry

        lax.fori_loop(0, ne, place, 0)
        v_re, v_im = coef_ref[0], coef_ref[1]
        energy = jnp.sum(v_re * v_re + v_im * v_im, axis=0, keepdims=True) / blocks
        factor = lax.rsqrt(energy + 1e-05)
        coef_ref[0] = v_re * factor
        coef_ref[1] = v_im * factor


def exchange_and_iterate(nq, ne, spec, own, weight, triad):
    blocks, bands, band, width = spec.shape
    cols = bands * band
    triads = triad.shape[1]
    pieces = 2 * (blocks // ne) * (triads // LANES)
    assert pieces == nq and LANES == 2 * nq and triads == 8 * nq
    f32, bf16 = jnp.float32, jnp.bfloat16
    vmem = pl.BlockSpec(memory_space=pltpu.VMEM)
    return pl.pallas_call(
        functools.partial(kernel, nq, ne),
        out_shape=(
            jax.ShapeDtypeStruct((2 * triads // nq, blocks), f32),
            jax.ShapeDtypeStruct(own.shape, bf16),
            jax.ShapeDtypeStruct((own.shape[1] // 2, own.shape[2] // 3), f32),
        ),
        in_specs=[vmem, vmem, pl.BlockSpec(memory_space=pltpu.SMEM), vmem],
        out_specs=(vmem, vmem, vmem),
        scratch_shapes=[
            pltpu.VMEM((ne, 1, LANES), f32),
            pltpu.VMEM((cols * blocks, LANES), f32),
            pltpu.VMEM((blocks, bands, band, width), bf16),
            pltpu.VMEM((width // LANES, blocks * 16, LANES), f32),
            pltpu.VMEM((cols * blocks, width), bf16),
            pltpu.VMEM((cols * blocks, triads), bf16),
            pltpu.VMEM((cols * blocks, triads), bf16),
            pltpu.VMEM((cols * blocks, triads), bf16),
            pltpu.VMEM((cols * blocks, triads), bf16),
            pltpu.VMEM((8, LANES), f32),
            pltpu.VMEM((2, blocks, triads), f32),
            pltpu.VMEM((2, triads // LANES, 2, blocks, LANES), f32),
            pltpu.VMEM((2, triads // LANES, ne, 2, blocks // ne, LANES), f32),
            pltpu.VMEM((2, pieces, 1, LANES), f32),
            pltpu.VMEM((2, nq, 1, LANES), f32),
            pltpu.VMEM((2, 1, LANES), f32),
            pltpu.VMEM((nq, 1, LANES), f32),
            pltpu.VMEM((ne, nq, 1, LANES), f32),
            pltpu.SemaphoreType.DMA((16,)),
            pltpu.SemaphoreType.DMA((16,)),
        ],
        compiler_params=pltpu.CompilerParams(
            collective_id=0, has_side_effects=True, vmem_limit_bytes=48 * 1024 * 1024
        ),
    )(spec, own, weight, triad)


def body(snapshots, point_weights, owner_map, triad_list):
    samples = snapshots.shape[1]
    points = snapshots.shape[3]
    columns = 3 * points
    frequencies = owner_map.shape[0]
    triad_count = triad_list.shape[0]
    nq, ne = lax.axis_size("freq"), lax.axis_size("space")
    triads_here = triad_count // nq
    slots = frequencies // nq
    per_slot = triads_here // slots
    mine = lax.axis_index("freq")
    table = make_table(samples, frequencies)
    data = snapshots.reshape(samples, columns)
    by_part = table.reshape(frequencies, 2, samples).transpose(1, 0, 2).reshape(2 * frequencies, samples)
    spec = lax.dot_general(
        data, by_part, (((0,), (1,)), ((), ())), preferred_element_type=jnp.float32
    ).astype(jnp.bfloat16)
    owned_table = select_rows(owner_map, table.reshape(frequencies, 2 * samples))
    own = jnp.dot(
        owned_table.astype(jnp.bfloat16).reshape(2 * frequencies, samples),
        data,
        preferred_element_type=jnp.float32,
    ).astype(jnp.bfloat16)
    cols = columns // nq
    first, second = triad_list[:, 0], triad_list[:, 1]
    triad = jnp.stack([first, second, first + second])
    triad = triad.reshape(3, nq, triads_here).transpose(0, 2, 1).reshape(3, triad_count)
    vec, sums, power_map = exchange_and_iterate(
        nq, ne, spec.reshape(nq, cols // 4, 4, 2 * frequencies), own.reshape(nq, 2 * slots, columns), point_weights, triad
    )
    coefficients = vec.reshape(triads_here, 2, nq)
    sums = sums.reshape(nq, slots, 2, columns)
    rounded = coefficients.astype(jnp.bfloat16).reshape(per_slot, slots, 2, nq)
    out = jnp.einsum("quxb,buyk->quxyk", rounded, sums, preferred_element_type=jnp.float32)
    mode_real = out[:, :, 0, 0] - out[:, :, 1, 1]
    mode_imag = out[:, :, 0, 1] + out[:, :, 1, 0]
    modes = jnp.stack([mode_real, mode_imag], axis=2) / math.sqrt(nq)
    return (power_map, coefficients, modes.reshape(triads_here, 2, 3, points))


def solution(mesh):
    placed = (P("freq", None, None, "space"), P("space"), P(), P())
    return jax.shard_map(
        body,
        mesh=mesh,
        in_specs=placed,
        out_specs=(P("freq", "space"), P("freq", None, None), P("freq", None, None, "space")),
        check_vma=False,
    )
```

```python
import functools
import math

import jax
import jax.numpy as jnp
from jax import lax
from jax.experimental import pallas as pl
from jax.experimental.pallas import tpu as pltpu
from jax.sharding import PartitionSpec as P


def make_table(samples, frequencies):
    sample_idx = jnp.arange(samples, dtype=jnp.int32)
    freq_idx = jnp.arange(frequencies, dtype=jnp.int32)
    angles = (freq_idx[:, None] * sample_idx[None, :] % samples).astype(jnp.float32) * (
        2.0 * math.pi / samples
    )
    window = 0.5 - 0.5 * jnp.cos(sample_idx.astype(jnp.float32) * (2.0 * math.pi / samples))
    taper = window / math.sqrt(samples)
    stacked = jnp.stack([jnp.cos(angles) * taper, -jnp.sin(angles) * taper], axis=1)
    return stacked.reshape(2 * frequencies, samples).astype(jnp.bfloat16)


def select_rows(index, rows):
    hot = (index[:, None] == jnp.arange(rows.shape[0], dtype=jnp.int32)[None, :]).astype(jnp.bfloat16)
    return jnp.dot(hot, rows, preferred_element_type=jnp.float32)


MESH = pl.DeviceIdType.MESH
LANES = 128


def kernel(
    nq, ne, spec_ref, own_ref, weight_ref, triad_ref,
    out_ref, sums_ref, power_ref,
    last_ref, weight_rows, spec_all, flat, rows, prod_re, prod_im, sum_re, sum_im, field,
    coef_ref, part, part_in, piece, piece_in, mine, gathered, spread,
    send_sem, recv_sem,
):
    q = lax.axis_index("freq")
    e = lax.axis_index("space")
    blocks, bands, band, width = spec_ref.shape
    cols = bands * band
    pad = flat.shape[1] // blocks
    triads = triad_ref.shape[1]
    per_e = blocks // ne
    groups = triads // LANES

    barrier = pltpu.get_barrier_semaphore()

    ring = 16

    def far_first(k, count):
        return (count // 2 + (1 - 2 * (k % 2)) * ((k + 1) // 2)) % count

    def others(axis, count, index, act):
        def step(k, carry):
            if axis == "freq":
                outer = count // ring
                far_z, far_y = far_first(k // outer, ring), far_first(k % outer, outer)
                i = (index // ring + far_y) % outer * ring + (index + far_z) % ring
            else:
                i = (index + far_first(k, count)) % count
            act({axis: i}, i)
            return carry

        lax.fori_loop(0, count - 1, step, 0)

    def greet(device, _):
        pl.semaphore_signal(barrier, inc=1, device_id=device, device_id_type=MESH)

    others("freq", nq, q, greet)
    others("space", ne, e, greet)
    for j in range(cols):
        value = weight_ref[(q * cols + j) % weight_ref.shape[0]]
        weight_rows[j * blocks : (j + 1) * blocks, :] = jnp.full((blocks, LANES), value)
    pl.semaphore_wait(barrier, nq + ne - 2)

    def exchange(slot, axis, count, index, source, target):
        def act(device, i):
            pltpu.make_async_remote_copy(
                src_ref=source(i), dst_ref=target.at[index],
                send_sem=send_sem.at[slot], recv_sem=recv_sem.at[slot],
                device_id=device, device_id_type=MESH,
            ).start()

        pltpu.make_async_copy(source(index), target.at[index], recv_sem.at[slot]).start()
        others(axis, count, index, act)

        def finish():
            pltpu.make_async_copy(target, target, recv_sem.at[slot]).wait()
            rest = target.at[pl.ds(0, count - 1)]
            pltpu.make_async_copy(rest, rest, send_sem.at[slot]).wait()

        return finish

    got_spec = exchange(0, "freq", nq, q, lambda i: spec_ref.at[i], spec_all)
    got_spec()

    def widen(b, carry):
        for k in range(bands):
            block = spec_all[b, k].astype(jnp.float32)
            there = pl.ds(b * pad + k * band, band)
            for h in range(width // LANES):
                flat[h, there, :] = block[:, h * LANES : (h + 1) * LANES]
        return carry

    lax.fori_loop(0, blocks, widen, 0)
    for j in range(cols):
        for h in range(width // LANES):
            rows[j * blocks : (j + 1) * blocks, h * LANES : (h + 1) * LANES] = flat[
                h, pl.ds(j, blocks, stride=pad), :
            ].astype(jnp.bfloat16)

    half = width // 2
    for c in range(triads // 256):
        lanes = slice(c * 256, (c + 1) * 256)
        at = lax.broadcasted_iota(jnp.int32, (width, 256), 0)

        def pick(row, shift):
            hot = jnp.where(at == triad_ref[row : row + 1, lanes] + shift, 1.0, 0.0)
            return hot.astype(jnp.bfloat16)

        hots = [pick(row, shift) for row in range(3) for shift in (0, half)]
        for j in range(0, cols, 2):
            here = slice(j * blocks, (j + 2) * blocks)
            k_re, k_im, l_re, l_im, s_re, s_im = [
                jnp.dot(rows[here, :], hot, preferred_element_type=jnp.float32) for hot in hots
            ]
            weight = weight_rows[here, :]
            weight = jnp.concatenate([weight, weight], axis=1)
            prod_re[here, lanes] = ((k_re * l_re - k_im * l_im) * weight).astype(jnp.bfloat16)
            prod_im[here, lanes] = ((k_re * l_im + k_im * l_re) * weight).astype(jnp.bfloat16)
            sum_re[here, lanes] = s_re.astype(jnp.bfloat16)
            sum_im[here, lanes] = s_im.astype(jnp.bfloat16)

    coef_ref[0] = jnp.ones((blocks, triads), jnp.float32)
    coef_ref[1] = jnp.zeros((blocks, triads), jnp.float32)

    for sweep in range(2):
        base = 2 + 7 * sweep
        got_parts = []
        for g in range(groups):
            lanes = slice(g * LANES, (g + 1) * LANES)
            a_re, a_im = coef_ref[0, :, lanes], coef_ref[1, :, lanes]

            def column(j, carry):
                v_re, v_im = carry
                here = pl.ds(pl.multiple_of(j * blocks, blocks), blocks)
                s_re = sum_re[here, lanes].astype(jnp.float32)
                s_im = sum_im[here, lanes].astype(jnp.float32)
                f_re = jnp.sum(a_re * s_re - a_im * s_im, axis=0, keepdims=True)
                f_im = jnp.sum(a_re * s_im + a_im * s_re, axis=0, keepdims=True)
                p_re = prod_re[here, lanes].astype(jnp.float32)
                p_im = prod_im[here, lanes].astype(jnp.float32)
                return (v_re + (p_re * f_re + p_im * f_im), v_im + (p_re * f_im - p_im * f_re))

            zero = jnp.zeros((blocks, LANES), jnp.float32)
            v_re, v_im = lax.fori_loop(0, cols, column, (zero, zero))
            part[sweep, g, 0] = v_re
            part[sweep, g, 1] = v_im
            got_parts.append(
                exchange(
                    base + g, "space", ne, e,
                    lambda i: part.at[sweep, g, :, pl.ds(pl.multiple_of(i * per_e, per_e), per_e), :],
                    part_in.at[sweep, g],
                )
            )

        for got_part in got_parts:
            got_part()
        totals = [jnp.sum(part_in[sweep, g], axis=0) for g in range(groups)]
        if sweep == 0:
            for r in range(2):
                for b in range(per_e):
                    for g in range(groups):
                        piece[sweep, (r * per_e + b) * groups + g] = totals[g][
                            r, b : b + 1
                        ]
        else:
            stack = jnp.concatenate(
                [totals[g][r] for g in range(groups) for r in range(2)], axis=0
            )
            blank = jnp.zeros_like(stack)
            even = jnp.concatenate([stack, blank], axis=0).T
            odd = jnp.concatenate([blank, stack], axis=0).T
            by_owner = even[:nq] + odd[nq:]
            for i in range(nq):
                piece[sweep, i] = by_owner[i : i + 1]
        got_piece = exchange(
            base + 4, "freq", nq, q, lambda i: piece.at[sweep, i], piece_in.at[sweep]
        )
        if sweep == 1:
            got_sums()

            def energy_of(b, total):
                values = sums_ref[b].astype(jnp.float32)
                return total + values * values

            energy = lax.fori_loop(0, blocks, energy_of, jnp.zeros(sums_ref.shape[1:], jnp.float32))
            points = power_ref.shape[1]
            for slot in range(power_ref.shape[0]):
                pair = energy[2 * slot : 2 * slot + 1] + energy[2 * slot + 1 : 2 * slot + 2]
                pair = pair[:, :points] + pair[:, points : 2 * points] + pair[:, 2 * points :]
                power_ref[slot : slot + 1, :] = pair / blocks
        got_piece()
        mine[sweep] = jnp.sum(piece_in[sweep], axis=0)
        if sweep == 1:
            exchange(base + 6, "space", ne, e, lambda i: mine.at[sweep], last_ref)()
            values = jnp.concatenate([last_ref[i] for i in range(ne)], axis=0)
            square = jnp.sum(values * values, axis=0, keepdims=True)
            share = 2 * per_e
            here = lax.broadcasted_iota(jnp.int32, (LANES, LANES), 0) // share
            there = lax.broadcasted_iota(jnp.int32, (LANES, LANES), 1) // share
            same = jnp.where(here == there, 1.0, 0.0)
            energy = jnp.dot(
                jnp.broadcast_to(square, (ne, LANES)), same,
                precision=lax.Precision.HIGHEST, preferred_element_type=jnp.float32,
            )
            values = values * lax.rsqrt(energy / blocks + 1e-05)
            lane = lax.broadcasted_iota(jnp.int32, (2 * triads // nq, LANES), 1)
            row_of = (2 * (lane // share % groups) + lane // nq) * 2 + lane // per_e % 2
            own_row = row_of == lax.broadcasted_iota(jnp.int32, row_of.shape, 0)
            wide = jnp.concatenate(
                [jnp.where(own_row, values[i : i + 1], 0.0) for i in range(ne)], axis=1
            )
            k = lax.broadcasted_iota(jnp.int32, (ne * LANES, LANES), 0)
            to = k // LANES * per_e + k % per_e
            there = jnp.where(to == lax.broadcasted_iota(jnp.int32, to.shape, 1), 1.0, 0.0)
            placed = jnp.dot(
                wide, there, precision=lax.Precision.HIGHEST, preferred_element_type=jnp.float32
            )
            out_ref[...] = placed[:, :blocks]
            break
        got_mine = exchange(base + 5, "freq", nq, q, lambda i: mine.at[sweep], gathered)
        got_mine()
        got_spread = exchange(base + 6, "space", ne, e, lambda i: gathered, spread)
        got_sums = exchange(1, "freq", nq, q, lambda i: own_ref.at[i], sums_ref)
        got_spread()

        def place(d, carry):
            for r in range(2):
                for g in range(groups):
                    block = jnp.concatenate(
                        [spread[d, (r * per_e + b) * groups + g] for b in range(per_e)], axis=0
                    )
                    there = pl.ds(pl.multiple_of(d * per_e, per_e), per_e)
                    coef_ref[r, there, g * LANES : (g + 1) * LANES] = block
            return carry

        lax.fori_loop(0, ne, place, 0)
        v_re, v_im = coef_ref[0], coef_ref[1]
        energy = jnp.sum(v_re * v_re + v_im * v_im, axis=0, keepdims=True) / blocks
        factor = lax.rsqrt(energy + 1e-05)
        coef_ref[0] = v_re * factor
        coef_ref[1] = v_im * factor


def exchange_and_iterate(nq, ne, spec, own, weight, triad):
    blocks, bands, band, width = spec.shape
    cols = bands * band
    triads = triad.shape[1]
    pieces = 2 * (blocks // ne) * (triads // LANES)
    assert pieces == nq and LANES == 2 * nq and triads == 8 * nq
    f32, bf16 = jnp.float32, jnp.bfloat16
    vmem = pl.BlockSpec(memory_space=pltpu.VMEM)
    return pl.pallas_call(
        functools.partial(kernel, nq, ne),
        out_shape=(
            jax.ShapeDtypeStruct((2 * triads // nq, blocks), f32),
            jax.ShapeDtypeStruct(own.shape, bf16),
            jax.ShapeDtypeStruct((own.shape[1] // 2, own.shape[2] // 3), f32),
        ),
        in_specs=[vmem, vmem, pl.BlockSpec(memory_space=pltpu.SMEM), vmem],
        out_specs=(vmem, vmem, vmem),
        scratch_shapes=[
            pltpu.VMEM((ne, 1, LANES), f32),
            pltpu.VMEM((cols * blocks, LANES), f32),
            pltpu.VMEM((blocks, bands, band, width), bf16),
            pltpu.VMEM((width // LANES, blocks * 16, LANES), f32),
            pltpu.VMEM((cols * blocks, width), bf16),
            pltpu.VMEM((cols * blocks, triads), bf16),
            pltpu.VMEM((cols * blocks, triads), bf16),
            pltpu.VMEM((cols * blocks, triads), bf16),
            pltpu.VMEM((cols * blocks, triads), bf16),
            pltpu.VMEM((8, LANES), f32),
            pltpu.VMEM((2, blocks, triads), f32),
            pltpu.VMEM((2, triads // LANES, 2, blocks, LANES), f32),
            pltpu.VMEM((2, triads // LANES, ne, 2, blocks // ne, LANES), f32),
            pltpu.VMEM((2, pieces, 1, LANES), f32),
            pltpu.VMEM((2, nq, 1, LANES), f32),
            pltpu.VMEM((2, 1, LANES), f32),
            pltpu.VMEM((nq, 1, LANES), f32),
            pltpu.VMEM((ne, nq, 1, LANES), f32),
            pltpu.SemaphoreType.DMA((16,)),
            pltpu.SemaphoreType.DMA((16,)),
        ],
        compiler_params=pltpu.CompilerParams(
            collective_id=0, has_side_effects=True, vmem_limit_bytes=48 * 1024 * 1024
        ),
    )(spec, own, weight, triad)


def body(snapshots, point_weights, owner_map, triad_list):
    samples = snapshots.shape[1]
    points = snapshots.shape[3]
    columns = 3 * points
    frequencies = owner_map.shape[0]
    triad_count = triad_list.shape[0]
    nq, ne = lax.axis_size("freq"), lax.axis_size("space")
    triads_here = triad_count // nq
    slots = frequencies // nq
    per_slot = triads_here // slots
    mine = lax.axis_index("freq")
    table = make_table(samples, frequencies)
    data = snapshots.reshape(samples, columns)
    by_part = table.reshape(frequencies, 2, samples).transpose(1, 0, 2).reshape(2 * frequencies, samples)
    spec = lax.dot_general(
        data, by_part, (((0,), (1,)), ((), ())), preferred_element_type=jnp.float32
    ).astype(jnp.bfloat16)
    owned_table = select_rows(owner_map, table.reshape(frequencies, 2 * samples))
    own = jnp.dot(
        owned_table.astype(jnp.bfloat16).reshape(2 * frequencies, samples),
        data,
        preferred_element_type=jnp.float32,
    ).astype(jnp.bfloat16)
    cols = columns // nq
    first, second = triad_list[:, 0], triad_list[:, 1]
    triad = jnp.stack([first, second, first + second])
    triad = triad.reshape(3, nq, triads_here).transpose(0, 2, 1).reshape(3, triad_count)
    vec, sums, power_map = exchange_and_iterate(
        nq, ne, spec.reshape(nq, cols // 4, 4, 2 * frequencies), own.reshape(nq, 2 * slots, columns), point_weights, triad
    )
    coefficients = vec.reshape(triads_here, 2, nq)
    sums = sums.reshape(nq, slots, 2, columns)
    rounded = coefficients.astype(jnp.bfloat16).reshape(per_slot, slots, 2, nq)
    out = jnp.einsum("quxb,buyk->quxyk", rounded, sums, preferred_element_type=jnp.float32)
    mode_real = out[:, :, 0, 0] - out[:, :, 1, 1]
    mode_imag = out[:, :, 0, 1] + out[:, :, 1, 0]
    modes = jnp.stack([mode_real, mode_imag], axis=2) / math.sqrt(nq)
    return (power_map, coefficients, modes.reshape(triads_here, 2, 3, points))


def solution(mesh):
    placed = (P("freq", None, None, "space"), P("space"), P(), P())
    return jax.shard_map(
        body,
        mesh=mesh,
        in_specs=placed,
        out_specs=(P("freq", "space"), P("freq", None, None), P("freq", None, None, "space")),
        check_vma=False,
    )
```
